256 devices in a mesh: gx: 32 (over x, y, core), gy: 8 (over z).
Axes of the slice: x: 4, y: 4, z: 8, core: 2. Of those that a mesh axis runs over, the one named last changes fastest.
Arguments:
- hidden: bfloat16 [1024, 16384], P('gx', 'gy'), may hold values from -40 to 40
- lm_head: bfloat16 [16384, 65536], P('gy', 'gx'), may hold values from -1 to 1
- parent: int32 [1024], replicated, may hold values from 0 to 1023, as said below
- draft_token: int32 [1024], replicated, may hold values from 0 to 65535
- draft_prob: float32 [1024], replicated, may hold values from 0.01 to 1
- uniforms: float32 [1024], replicated, may hold values from 0.01 to 1
- node_count: int32 [16], replicated, may hold values from 1 to 64, as said below
- accepted_end: int32 [16], replicated, may hold values from 0 to 63, as said below
Outputs:
- vertex_accept_slack: float32 [1024], P('gx')
- lineage_least_slack: float32 [1024], P('gx')
- extra_draw_score: float32 [16, 65536], P(None, 'gx')
The draws below stay inside these ranges and needn't reach their ends.
Inputs may be any that keep to these rules, and one draw needn't show every extreme that they name: A node's parent lies in the same sequence at a lower slot; slot 0 of each sequence is its own parent. `node_count`: some sequence has all 64 slots live. `accepted_end`: the slot of a live node of that sequence.
All inputs are finite; a program needn't handle non-finite values.
Results may differ from the reference program's by a relative error of at most 0.0003.
Values may be sent and summed in bfloat16 or wider, within the bound.
A program may use at most 64 MiB of HBM per device.

```python
import math
import jax
import jax.numpy as jnp

D = 16384
VOCAB = 65536
TREE = 64
NODES = 1024
SEQS = 16


def draw_hidden(key, part):
    scale_key = jax.random.fold_in(key, 11)
    value_key = jax.random.fold_in(key, 12)
    base = jnp.clip(jax.random.normal(value_key, (NODES, D), jnp.float32), -6.0, 6.0)
    scales = jnp.exp(jax.random.uniform(scale_key, (NODES, 1), jnp.float32, jnp.log(0.5), jnp.log(5.0)))
    values = base * scales
    return values.astype(jnp.bfloat16)


def draw_lm_head(key, part):
    scale_key = jax.random.fold_in(key, 21)
    value_key = jax.random.fold_in(key, 22)
    col_scales = jnp.exp(jax.random.uniform(scale_key, (1, VOCAB), jnp.float32, jnp.log(0.3), jnp.log(3.0)))
    spread = 3.0 / D ** 0.5
    base = jnp.clip(jax.random.normal(value_key, (D, VOCAB), jnp.float32), -6.0, 6.0)
    values = base * spread * col_scales
    return values.astype(jnp.bfloat16)


def draw_parent(key, part):
    node_index = jnp.arange(NODES, dtype=jnp.int32)
    local_index = node_index % TREE
    lowest = jnp.maximum(local_index - 4, 0)
    highest = jnp.maximum(local_index, 1)
    chosen = jax.random.randint(jax.random.fold_in(key, 31), (NODES,), lowest, highest)
    chosen = jnp.where(local_index == 0, 0, chosen)
    return (node_index - local_index + chosen).astype(jnp.int32)


def counts_and_ends(key):
    base_key = jax.random.fold_in(key, 41)
    counts = jax.random.randint(jax.random.fold_in(base_key, 1), (SEQS,), 1, TREE + 1)
    full_seq = jax.random.randint(jax.random.fold_in(base_key, 2), (), 0, SEQS)
    counts = counts.at[full_seq].set(TREE)
    end_slots = jax.random.randint(jax.random.fold_in(base_key, 3), (SEQS,), 0, counts)
    end_slots = end_slots.at[full_seq].set(TREE - 1)
    end_slots = end_slots.at[(full_seq + 1) % SEQS].set(0)
    return (counts.astype(jnp.int32), end_slots.astype(jnp.int32))


def draw_node_count(key, part):
    return counts_and_ends(key)[0]


def draw_accepted_end(key, part):
    return counts_and_ends(key)[1]


def plant(values, rng, least, top_value):
    longest = values.shape.index(max(values.shape))
    spots = []
    for shift in (0, 1):
        where = [jax.random.randint(jax.random.fold_in(rng, axis), (), 0, length) for axis, length in enumerate(values.shape)]
        where[longest] = (where[longest] + shift) % values.shape[longest]
        spots.append(tuple(where))
    return values.at[spots[0]].set(least).at[spots[1]].set(top_value)


def setup_inputs(seed: int = 0) -> dict:
    splits = jax.random.split(jax.random.key(seed), 9)
    hidden = draw_hidden(jax.random.fold_in(splits[8], 71), 0)
    lm_head = draw_lm_head(jax.random.fold_in(splits[8], 71), 0)
    parent = draw_parent(jax.random.fold_in(splits[8], 71), 0)
    draft_token = plant(jax.random.randint(splits[3], (NODES,), 0, VOCAB), jax.random.fold_in(splits[3], 1), 0, VOCAB - 1).astype(jnp.int32)
    draft_prob = jnp.clip(jnp.exp(jax.random.uniform(splits[4], (NODES,), jnp.float32, math.log(0.01), math.log(1.0))), 0.01, 1.0)
    uniforms = jnp.clip(jax.random.uniform(splits[5], (NODES,), jnp.float32, 0.01, 1.0), 0.01, 1.0)
    node_count = draw_node_count(jax.random.fold_in(splits[8], 71), 0)
    accepted_end = draw_accepted_end(jax.random.fold_in(splits[8], 71), 0)
    return {"hidden": hidden, "lm_head": lm_head, "parent": parent, "draft_token": draft_token, "draft_prob": draft_prob, "uniforms": uniforms, "node_count": node_count, "accepted_end": accepted_end}


big_margin = 10000.0


def reference(hidden, lm_head, parent, draft_token, draft_prob, uniforms, node_count, accepted_end):
    emitted_scores = jnp.dot(hidden, lm_head, preferred_element_type=jnp.float32)
    row_max = jnp.max(emitted_scores, axis=1)
    partition_function = row_max + jnp.log(jnp.sum(jnp.exp(emitted_scores - row_max[:, None]), axis=1))
    target = emitted_scores[parent, draft_token]
    margin = target - partition_function[parent] - jnp.log(draft_prob) - jnp.log(uniforms)
    node_index = jnp.arange(NODES, dtype=jnp.int32)
    local_index = node_index % TREE
    live_mask = local_index < node_count[node_index // TREE]
    root_mask = parent == node_index
    spare_mask = jnp.logical_or(root_mask, jnp.logical_not(live_mask))
    vertex_accept_slack = jnp.where(spare_mask, jnp.float32(0.0), margin)
    path_min = jnp.where(root_mask, jnp.float32(big_margin), margin)
    ancestor = parent
    for _ in range((TREE - 1).bit_length()):
        path_min = jnp.minimum(path_min, path_min[ancestor])
        ancestor = ancestor[ancestor]
    lineage_least_slack = jnp.where(spare_mask, jnp.float32(0.0), path_min)
    leaf_entries = jnp.arange(SEQS, dtype=jnp.int32) * TREE + accepted_end
    extra_draw_score = emitted_scores[leaf_entries] - partition_function[leaf_entries][:, None]
    return vertex_accept_slack, lineage_least_slack, extra_draw_score
```

```python
import functools

import jax
import jax.numpy as jnp
from jax import lax
from jax.experimental import pallas as pl
from jax.experimental.pallas import tpu as pltpu
from jax.sharding import Mesh
from jax.sharding import PartitionSpec as P

GX = ("gx_0", "gx_1", "gx_2")
ALL = ("gx_0", "gx_1", "gx_2", "gy")
NX, NY, NC, NZ = 4, 4, 2, 8
PLANE = NX * NY * NC
HALF = 16
TILE = 256
BLOCKS = (48, 64, 128)
BIG = 10000.0
F32 = jnp.float32
BF16 = jnp.bfloat16
AT = pl.DeviceIdType.MESH


def iota(shape, dim):
    return lax.broadcasted_iota(jnp.int32, shape, dim)


def to_column(row, rows):
    spread = jnp.broadcast_to(row, (rows, row.shape[1]))
    keep = iota(spread.shape, 0) == iota(spread.shape, 1)
    return jnp.sum(jnp.where(keep, spread, 0.0), axis=1, keepdims=True)


def to_row(column, lanes):
    spread = jnp.broadcast_to(column, (column.shape[0], lanes))
    keep = iota(spread.shape, 0) == iota(spread.shape, 1)
    return jnp.sum(jnp.where(keep, spread, 0.0), axis=0, keepdims=True)


def two_rows(first, second):
    lines = iota((16, first.shape[1]), 0)
    return jnp.where(lines == 0, first, jnp.where(lines == 1, second, 0.0)).astype(BF16)


def kernel(
    cap, vec, own, head, out_s, out_e,
    w, hid, comp, acc, pick, tok, rank, pos, pp, reach, rq, rs, sq, ss,
    scores, tpk, send_a, recv_a, send_b, recv_b, ext,
    loc, gs, gr, pr, qs, qr, ps, pq, a_s, a_r, b_s, b_r, e_s, e_r,
):
    rows = cap * NZ
    nodes = vec.shape[1]
    width = head.shape[1]
    tiles = width // TILE
    x, y = lax.axis_index("gx_0"), lax.axis_index("gx_1")
    c, z = lax.axis_index("gx_2"), lax.axis_index("gy")
    gx = (x * NY + y) * NC + c
    first = c == 0

    def plane_peer(k):
        p = lax.rem(gx + k, PLANE)
        return p, (p // (NY * NC), lax.rem(p // NC, NY), lax.rem(p, NC), z)

    def z_peer(k):
        p = lax.rem(z + k, NZ)
        return p, (x, y, c, p)

    load_w = pltpu.make_async_copy(head, w, loc.at[0])
    load_w.start()

    def block(da, db, h, core):
        straight = core == 0
        bx = lax.rem(x + jnp.where(straight, da, db), NX)
        by = lax.rem(y + jnp.where(straight, db, da), NY)
        at = (((bx * NY + by) * NC + core) * 2 + h) * HALF
        return pl.ds(pl.multiple_of(at, HALF), HALF)

    own_rows = pl.ds(pl.multiple_of(gx * 2 * HALF, 2 * HALF), 2 * HALF)
    load_own = pltpu.make_async_copy(own, hid.at[own_rows], loc.at[1])
    load_own.start()

    barrier = pltpu.get_barrier_semaphore()

    def greet_plane(k, _):
        pl.semaphore_signal(barrier, inc=1, device_id=plane_peer(k)[1], device_id_type=AT)
        return 0

    def greet_z(k, _):
        pl.semaphore_signal(barrier, inc=1, device_id=z_peer(k)[1], device_id_type=AT)
        return 0

    lax.fori_loop(1, PLANE, greet_plane, 0)
    lax.fori_loop(1, NZ, greet_z, 0)
    load_own.wait()
    pl.semaphore_wait(barrier, PLANE - 1 + NZ - 1)

    sent = {0: [], 1: []}

    def chip(axis, step):
        along_x = first if axis == 0 else jnp.logical_not(first)
        tx = lax.rem(x + jnp.where(along_x, step, 0) + NX, NX)
        ty = lax.rem(y + jnp.where(along_x, 0, step) + NY, NY)
        return (tx, ty, c, z)

    def send(da, db, h, axis, step):
        here = block(da, db, h, c)
        ra = (da - step) % 4 if axis == 0 else da
        rb = (db - step) % 4 if axis == 1 else db
        copy = pltpu.make_async_remote_copy(
            src_ref=hid.at[here], dst_ref=hid.at[here],
            send_sem=gs.at[h, len(sent[h])], recv_sem=gr.at[h, ra, rb],
            device_id=chip(axis, step), device_id_type=AT,
        )
        copy.start()
        sent[h].append(copy)

    def share(da, db, h):
        here = block(da, db, h, c)
        copy = pltpu.make_async_remote_copy(
            src_ref=hid.at[here], dst_ref=hid.at[here],
            send_sem=gs.at[h, len(sent[h])], recv_sem=pr.at[h, da, db],
            device_id=(x, y, 1 - c, z), device_id_type=AT,
        )
        copy.start()
        sent[h].append(copy)

    def arrive(da, db, h):
        here = block(da, db, h, c)
        pltpu.make_async_remote_copy(
            src_ref=hid.at[here], dst_ref=hid.at[here],
            send_sem=gs.at[h, 0], recv_sem=gr.at[h, da, db],
            device_id=(x, y, 1 - c, z), device_id_type=AT,
        ).wait_recv()

    def arrive_group(dx):
        for h in range(2):
            for k in range(4):
                da = jnp.where(first, k, dx)
                db = jnp.where(first, dx, k)
                here = block(da, db, h, 1 - c)
                pltpu.make_async_remote_copy(
                    src_ref=hid.at[here], dst_ref=hid.at[here],
                    send_sem=gs.at[h, 0], recv_sem=pr.at[h, da, db],
                    device_id=(x, y, 1 - c, z), device_id_type=AT,
                ).wait_recv()

    sign = (1, -1)
    for h in range(2):
        send(0, 0, h, 0, 1)
        send(0, 0, h, 0, -1)
        send(0, 0, h, 1, 1)
        send(0, 0, h, 1, -1)
        share(0, 0, h)

    quota = vec[2:3, :]
    lhs = two_rows(quota, quota)

    def count(j, _):
        lane = pl.ds(pl.multiple_of(j * 128, 128), 128)
        before = (iota((nodes, 128), 0) < iota((nodes, 128), 1) + j * 128).astype(F32).astype(BF16)
        rank[:, lane] = jnp.dot(lhs, before, preferred_element_type=F32)
        return 0

    lax.fori_loop(0, nodes // 128, count, 0)
    per = cap - 2
    order = rank[0:1, :]
    home = jnp.zeros_like(order)
    for i in range(1, NZ):
        home = home + (order >= float(i * per)).astype(F32)
    spot = home * cap + (order - home * per) + 2.0
    ends = vec[3:4, :]
    pair = jnp.floor(ends * 0.5)
    end_spot = jnp.where(ends >= 0.0, pair * cap + (ends - 2.0 * pair), -1.0)
    pos[...] = jnp.where(quota > 0.0, spot, end_spot)

    for h in range(2):
        s = sign[h]
        for da, db in ((3, 0), (1, 0), (0, 3), (0, 1)):
            arrive(da, db, h)
            if db == 0:
                if da == (-s) % 4:
                    send(da, db, h, 0, s)
                send(da, db, h, 1, 1)
                send(da, db, h, 1, -1)
            elif db == (-s) % 4:
                send(da, db, h, 1, s)
            share(da, db, h)

    def mark(j, _):
        at = pl.ds(pl.multiple_of(j * 128, 128), 128)
        pick[at, :] = (iota((128, nodes), 0) + j * 128 == pos[...].astype(jnp.int32)).astype(F32).astype(BF16)
        return 0

    lax.fori_loop(0, rows // 128, mark, 0)

    for h in range(2):
        s = sign[h]
        arrive(2, 0, h)
        send(2, 0, h, 1, 1)
        send(2, 0, h, 1, -1)
        share(2, 0, h)
        for da in (3, 1):
            for db in (3, 1):
                arrive(da, db, h)
                if db == (-s) % 4:
                    send(da, db, h, 1, s)
                share(da, db, h)
        arrive(0, 2, h)
        share(0, 2, h)

    def select(dx, start, last):
        arrive_group(dx)
        bx = lax.rem(x + dx, NX)
        part = pl.ds(pl.multiple_of(bx * (nodes // NX), nodes // NX), nodes // NX)

        def body(j, _):
            lane = pl.ds(pl.multiple_of(j * TILE, TILE), TILE)
            got = jnp.dot(pick[:, part], hid[part, lane], preferred_element_type=F32)
            if not start:
                got = got + acc[:, lane]
            if last:
                comp[:, lane] = got.astype(BF16)
            else:
                acc[:, lane] = got
            return 0

        lax.fori_loop(0, hid.shape[1] // TILE, body, 0)

    select(0, True, False)

    for h in range(2):
        s = sign[h]
        for db in (3, 1):
            arrive(2, db, h)
            if db == (-s) % 4:
                send(2, db, h, 1, s)
            share(2, db, h)
        for da in (3, 1):
            arrive(da, 2, h)
            share(da, 2, h)
    select(3, False, False)
    for h in range(2):
        arrive(2, 2, h)
        share(2, 2, h)
    select(1, False, False)

    def token_rows(j, _):
        at = pl.ds(pl.multiple_of(j * 128, 128), 128)
        mine = vec[1:2, :].astype(jnp.int32) - gx * width
        tok[at, :] = (iota((128, nodes), 0) + j * 128 == mine).astype(F32).astype(BF16)
        return 0

    lax.fori_loop(0, width // 128, token_rows, 0)
    upper = jnp.floor(pos[...] * (1.0 / 32.0))
    lhs = two_rows(upper, pos[...] - 32.0 * upper)

    def parent_place(j, _):
        lane = pl.ds(pl.multiple_of(j * 128, 128), 128)
        hit = (iota((nodes, 128), 0) == vec[0:1, lane].astype(jnp.int32)).astype(F32).astype(BF16)
        got = jnp.dot(lhs, hit, preferred_element_type=F32)
        pp[:, lane] = got[0:1, :] * 32.0 + got[1:2, :]
        return 0

    lax.fori_loop(0, nodes // 128, parent_place, 0)
    group = gx // 4
    mine = pl.ds(pl.multiple_of(group * 128, 128), 128)
    up = vec[0:1, mine].astype(jnp.int32) - group * 128
    line, lane_ids = iota((128, 128), 0), iota((128, 128), 1)
    reach[...] = jnp.where(line == up, 1.0, jnp.where(line == lane_ids, 1.0, 0.0))

    def spread(_, carry):
        now = reach[...].astype(BF16)
        reach[...] = jnp.minimum(jnp.dot(now, now, preferred_element_type=F32), 1.0)
        return carry

    lax.fori_loop(0, 6, spread, 0)

    load_w.wait()
    select(2, False, True)

    def quantize(v, k, j):
        top = jnp.maximum(jnp.max(jnp.abs(v), axis=0, keepdims=True), 1e-30)
        ss[k, j] = top * (1.0 / 32767.0)
        sq[k, j] = jnp.round(v * (32767.0 / top)).astype(jnp.int32).astype(jnp.int16)

    def ring_copies(k, j, way):
        to = (x, y, c, lax.rem(z + (1 if way == 0 else NZ - 1), NZ))
        return (
            pltpu.make_async_remote_copy(
                src_ref=sq.at[k, j], dst_ref=rq.at[k, j], send_sem=qs.at[k, j],
                recv_sem=qr.at[k, j], device_id=to, device_id_type=AT),
            pltpu.make_async_remote_copy(
                src_ref=ss.at[k, j], dst_ref=rs.at[k, j], send_sem=ps.at[k, j],
                recv_sem=pq.at[k, j], device_id=to, device_id_type=AT),
        )

    def lanes_of(j):
        return pl.ds(pl.multiple_of(j * TILE, TILE), TILE)

    def rows_of(step, way):
        d = lax.rem(z + (NZ - step if way == 0 else step), NZ)
        return pl.ds(pl.multiple_of(d * cap, 16), cap)

    def arrived(k, j, way):
        for copy in ring_copies(k, j, way):
            copy.wait_recv()
        return rq[k, j].astype(jnp.int32).astype(F32) * rs[k, j]

    def multiply(jj, _):
        for way in range(2):
            j = jj * 2 + way
            acc[:, lanes_of(j)] = jnp.dot(comp[...], w[:, lanes_of(j)], preferred_element_type=F32)
            quantize(acc[rows_of(1, way), lanes_of(j)], 0, j)
            for copy in ring_copies(0, j, way):
                copy.start()
        return 0

    lax.fori_loop(0, tiles // 2, multiply, 0)

    def ring(step, _):
        def tile(jj, _):
            for way in range(2):
                j = jj * 2 + way
                v = arrived(step - 2, j, way) + acc[rows_of(step, way), lanes_of(j)]
                quantize(v, step - 1, j)
                for copy in ring_copies(step - 1, j, way):
                    copy.start()
            return 0

        lax.fori_loop(0, tiles // 2, tile, 0)
        return 0

    lax.fori_loop(2, NZ, ring, 0)

    tpk[...] = jnp.zeros_like(tpk)

    def finish(jj, _):
        for way in range(2):
            j = jj * 2 + way
            v = arrived(NZ - 2, j, way) + acc[rows_of(0, way), lanes_of(j)]
            scores[:, lanes_of(j)] = v
            high = v.astype(BF16)
            rest = v - high.astype(F32)
            middle = rest.astype(BF16)
            low = (rest - middle.astype(F32)).astype(BF16)
            at = pl.ds(pl.multiple_of(j * TILE, TILE), TILE)
            got = jnp.dot(jnp.concatenate([high, middle, low], axis=0), tok[at, :], preferred_element_type=F32)
            tpk[...] += got[0:cap] + got[cap : 2 * cap] + got[2 * cap : 3 * cap]
        return 0

    lax.fori_loop(0, tiles // 2, finish, 0)

    ext[z] = scores[0:2, :]

    def ext_copy(k):
        p, to = z_peer(k)
        return pltpu.make_async_remote_copy(
            src_ref=ext.at[z], dst_ref=ext.at[z], send_sem=e_s.at[k],
            recv_sem=e_r.at[z], device_id=to, device_id_type=AT)

    def ext_start(k, _):
        ext_copy(k).start()
        return 0

    lax.fori_loop(1, NZ, ext_start, 0)

    top = jnp.max(scores[...], axis=1, keepdims=True)
    total = jnp.sum(jnp.exp(scores[...] - top), axis=1, keepdims=True)
    top_row, total_row = to_row(top, 128), to_row(total, 128)
    base = (z * cap).astype(F32)
    held = iota((cap, nodes), 0).astype(F32) + base == pp[...]
    target = jnp.sum(jnp.where(held, tpk[...], 0.0), axis=0, keepdims=True)
    for t in range(nodes // 128):
        send_a[t] = jnp.concatenate([target[:, t * 128 : (t + 1) * 128], top_row, total_row], axis=1)
    recv_a[gx] = send_a[group]

    def plane_copy(k):
        p, to = plane_peer(k)
        return pltpu.make_async_remote_copy(
            src_ref=send_a.at[p // 4], dst_ref=recv_a.at[gx], send_sem=a_s.at[k],
            recv_sem=a_r.at[gx], device_id=to, device_id_type=AT)

    def plane_start(k, _):
        plane_copy(k).start()
        return 0

    def plane_wait(k, _):
        p, to = plane_peer(k)
        pltpu.make_async_remote_copy(
            src_ref=send_a.at[0], dst_ref=recv_a.at[p], send_sem=a_s.at[k],
            recv_sem=a_r.at[p], device_id=to, device_id_type=AT).wait_recv()
        return 0

    lax.fori_loop(1, PLANE, plane_start, 0)
    lax.fori_loop(1, PLANE, plane_wait, 0)
    parts = [recv_a[k] for k in range(PLANE)]
    tops = [p[:, 128:256] for p in parts]
    while len(tops) > 1:
        tops = [jnp.maximum(a, b) for a, b in zip(tops[::2], tops[1::2])]
    sums = [p[:, 256:384] * jnp.exp(p[:, 128:256] - tops[0]) for p in parts]
    wanted = [p[:, 0:128] for p in parts]
    while len(sums) > 1:
        sums = [a + b for a, b in zip(sums[::2], sums[1::2])]
        wanted = [a + b for a, b in zip(wanted[::2], wanted[1::2])]
    used = iota((1, 128), 1) < cap
    log_total = jnp.where(used, tops[0] + jnp.log(jnp.where(used, sums[0], 1.0)), 0.0)
    column = to_column(log_total, cap)
    here = iota((cap, 128), 0).astype(F32) + base == pp[:, mine]
    mine_part = wanted[0] - jnp.sum(jnp.where(here, column, 0.0), axis=0, keepdims=True)
    send_b[...] = jnp.concatenate([mine_part, log_total], axis=1)
    recv_b[z] = send_b[...]

    def b_copy(k):
        p, to = z_peer(k)
        return pltpu.make_async_remote_copy(
            src_ref=send_b, dst_ref=recv_b.at[z], send_sem=b_s.at[k],
            recv_sem=b_r.at[z], device_id=to, device_id_type=AT)

    def b_start(k, _):
        b_copy(k).start()
        return 0

    def z_wait(k, _):
        p, to = z_peer(k)
        pltpu.make_async_remote_copy(
            src_ref=send_b, dst_ref=recv_b.at[p], send_sem=b_s.at[k],
            recv_sem=b_r.at[p], device_id=to, device_id_type=AT).wait_recv()
        pltpu.make_async_remote_copy(
            src_ref=ext.at[z], dst_ref=ext.at[p], send_sem=e_s.at[k],
            recv_sem=e_r.at[p], device_id=to, device_id_type=AT).wait_recv()
        return 0

    lax.fori_loop(1, NZ, b_start, 0)
    lax.fori_loop(1, NZ, z_wait, 0)

    margin = recv_b[0][:, 0:128]
    for k in range(1, NZ):
        margin = margin + recv_b[k][:, 0:128]
    margin = margin - vec[6:7, mine]
    spare = vec[4:5, mine] > 0.0
    climb = to_column(jnp.where(vec[5:6, mine] > 0.0, BIG, margin), 128)
    least = jnp.min(jnp.where(reach[...] > 0.0, climb, BIG), axis=0, keepdims=True)
    both = jnp.where(
        iota((8, 128), 0) == 0,
        jnp.where(spare, 0.0, margin),
        jnp.where(spare, 0.0, least),
    )
    out_s[...] = pltpu.roll(both, lax.rem(128 - 2 * HALF * lax.rem(gx, 4), 128), axis=1)
    lane = iota((1, 128), 1)
    for k in range(NZ):
        line = recv_b[k][:, 128:256]
        low = jnp.sum(jnp.where(lane == 0, line, 0.0), axis=1, keepdims=True)
        high = jnp.sum(jnp.where(lane == 1, line, 0.0), axis=1, keepdims=True)
        out_e[2 * k : 2 * k + 2, :] = ext[k] - jnp.where(iota((2, 1), 0) == 0, low, high)

    for h in range(2):
        for copy in sent[h]:
            copy.wait_send()

    def ring_drain(k, _):
        def tile(jj, _):
            for way in range(2):
                for copy in ring_copies(k, jj * 2 + way, way):
                    copy.wait_send()
            return 0

        lax.fori_loop(0, tiles // 2, tile, 0)
        return 0

    def plane_drain(k, _):
        plane_copy(k).wait_send()
        return 0

    def z_drain(k, _):
        ext_copy(k).wait_send()
        b_copy(k).wait_send()
        return 0

    lax.fori_loop(0, NZ - 1, ring_drain, 0)
    lax.fori_loop(1, PLANE, plane_drain, 0)
    lax.fori_loop(1, NZ, z_drain, 0)


def fused(cap, number, vec, hidden, head):
    depth, width = head.shape
    nodes = vec.shape[1]
    rows, tiles, hops = cap * NZ, width // TILE, NZ - 1
    dma = pltpu.SemaphoreType.DMA
    return pl.pallas_call(
        functools.partial(kernel, cap),
        out_shape=(
            jax.ShapeDtypeStruct((8, 128), F32),
            jax.ShapeDtypeStruct((2 * NZ, width), F32),
        ),
        in_specs=[
            pl.BlockSpec(memory_space=pltpu.VMEM),
            pl.BlockSpec(memory_space=pl.ANY),
            pl.BlockSpec(memory_space=pl.ANY),
        ],
        out_specs=(pl.BlockSpec(memory_space=pltpu.VMEM), pl.BlockSpec(memory_space=pltpu.VMEM)),
        scratch_shapes=[
            pltpu.VMEM((depth, width), BF16),
            pltpu.VMEM((nodes, depth), BF16),
            pltpu.VMEM((rows, depth), BF16),
            pltpu.VMEM((rows, width), F32),
            pltpu.VMEM((rows, nodes), BF16),
            pltpu.VMEM((width, nodes), BF16),
            pltpu.VMEM((16, nodes), F32),
            pltpu.VMEM((1, nodes), F32),
            pltpu.VMEM((1, nodes), F32),
            pltpu.VMEM((128, 128), F32),
            pltpu.VMEM((hops, tiles, cap, TILE), jnp.int16),
            pltpu.VMEM((hops, tiles, 1, TILE), F32),
            pltpu.VMEM((hops, tiles, cap, TILE), jnp.int16),
            pltpu.VMEM((hops, tiles, 1, TILE), F32),
            pltpu.VMEM((cap, width), F32),
            pltpu.VMEM((cap, nodes), F32),
            pltpu.VMEM((nodes // 128, 1, 384), F32),
            pltpu.VMEM((PLANE, 1, 384), F32),
            pltpu.VMEM((1, 256), F32),
            pltpu.VMEM((NZ, 1, 256), F32),
            pltpu.VMEM((NZ, 2, width), F32),
            dma((2,)),
            dma((2, 31)),
            dma((2, 4, 4)),
            dma((2, 4, 4)),
            dma((hops, tiles)),
            dma((hops, tiles)),
            dma((hops, tiles)),
            dma((hops, tiles)),
            dma((PLANE,)),
            dma((PLANE,)),
            dma((NZ,)),
            dma((NZ,)),
            dma((NZ,)),
            dma((NZ,)),
        ],
        compiler_params=pltpu.CompilerParams(
            collective_id=number, has_side_effects=True, vmem_limit_bytes=67043328
        ),
        name=f"head_{cap}",
    )(vec, hidden, head)


def local(hidden, lm_head, parent, draft_token, draft_prob, uniforms, node_count, accepted_end):
    nodes, seqs = parent.shape[0], node_count.shape[0]
    tree = nodes // seqs

    def per_node(a):
        return jnp.broadcast_to(a[:, None], (seqs, tree)).reshape(nodes)

    node = jnp.arange(nodes, dtype=jnp.int32)
    slot = node % tree
    live = slot < per_node(node_count)
    root = parent == node
    active = live & ~root
    needed = jnp.any((parent[None, :] == node[:, None]) & active[None, :], axis=1)
    end = slot == per_node(accepted_end)
    plain = needed & ~end
    vec = jnp.stack([
        parent.astype(F32),
        draft_token.astype(F32),
        plain.astype(F32),
        jnp.where(end, node // tree, -1).astype(F32),
        (root | ~live).astype(F32),
        root.astype(F32),
        jnp.log(draft_prob) + jnp.log(uniforms),
        jnp.zeros((nodes,), F32),
    ])
    size = jnp.sum(plain.astype(jnp.int32))
    which = sum((size > NZ * (cap - 2)).astype(jnp.int32) for cap in BLOCKS[:-1])
    branches = [functools.partial(fused, cap, i) for i, cap in enumerate(BLOCKS)]
    small, extra = lax.switch(which, branches, vec, hidden, lm_head)
    held = hidden.shape[0]
    return small[0, :held], small[1, :held], extra


def solution(mesh):
    finer = Mesh(mesh.devices.reshape(NX, NY, NC, NZ), ALL)
    placed = (P(GX, "gy"), P("gy", GX), P(), P(), P(), P(), P(), P())
    return jax.shard_map(
        local, mesh=finer, in_specs=placed, out_specs=(P(GX), P(GX), P(None, GX)), check_vma=False
    )
```

```python
import functools

import jax
import jax.numpy as jnp
from jax import lax
from jax.experimental import pallas as pl
from jax.experimental.pallas import tpu as pltpu
from jax.sharding import Mesh
from jax.sharding import PartitionSpec as P

GX = ("gx_0", "gx_1", "gx_2")
ALL = ("gx_0", "gx_1", "gx_2", "gy")
NX, NY, NC, NZ = 4, 4, 2, 8
PLANE = NX * NY * NC
HALF = 16
TILE = 256
LONG = 4
BLOCKS = (48, 64, 128)
BIG = 10000.0
F32 = jnp.float32
BF16 = jnp.bfloat16
AT = pl.DeviceIdType.MESH


def iota(shape, dim):
    return lax.broadcasted_iota(jnp.int32, shape, dim)


def to_column(row, rows):
    spread = jnp.broadcast_to(row, (rows, row.shape[1]))
    keep = iota(spread.shape, 0) == iota(spread.shape, 1)
    return jnp.sum(jnp.where(keep, spread, 0.0), axis=1, keepdims=True)


def to_row(column, lanes):
    spread = jnp.broadcast_to(column, (column.shape[0], lanes))
    keep = iota(spread.shape, 0) == iota(spread.shape, 1)
    return jnp.sum(jnp.where(keep, spread, 0.0), axis=0, keepdims=True)


def two_rows(first, second):
    lines = iota((16, first.shape[1]), 0)
    return jnp.where(lines == 0, first, jnp.where(lines == 1, second, 0.0)).astype(BF16)


def plan(parent, counts, ends, token, prob, uniform, vec, which):
    shape = parent.shape
    lines, lanes = iota((1, 128), 0), iota((1, 128), 1)
    total = jnp.zeros((1, 128), F32)
    before = (iota((128, 128), 0) < iota((128, 128), 1)).astype(F32).astype(BF16)
    order, reads = [], []
    for t in range(shape[0]):
        second = lanes >= 64
        slot = jnp.where(second, lanes - 64, lanes)
        live = slot < jnp.where(second, counts[2 * t + 1], counts[2 * t])
        end = slot == jnp.where(second, ends[2 * t + 1], ends[2 * t])
        up = parent[t : t + 1, :] - t * 128
        root = up == lanes
        child = jnp.where(live & jnp.logical_not(root), up.astype(F32), -1.0)
        column = to_column(child, 128)
        hit = (column == iota((128, 128), 1).astype(F32)).astype(F32)
        needed = jnp.max(hit, axis=0, keepdims=True)
        plain = jnp.where(end, 0.0, needed)
        vec[0 + t : 1 + t, :] = up.astype(F32)
        vec[16 + t : 17 + t, :] = plain
        vec[24 + t : 25 + t, :] = jnp.where(end, jnp.where(second, 2 * t + 1, 2 * t), -1).astype(F32)
        vec[32 + t : 33 + t, :] = jnp.where(root, 1.0, jnp.where(live, 0.0, 1.0))
        vec[40 + t : 41 + t, :] = root.astype(F32)
        within = jnp.dot(
            jnp.broadcast_to(plain, (16, 128)).astype(BF16), before, preferred_element_type=F32
        )[0:1, :]
        vec[56 + t : 57 + t, :] = within + total
        total = total + jnp.sum(plain, axis=1, keepdims=True)
    vec[8:16, :] = token[...].astype(F32)
    vec[48:56, :] = jnp.log(prob[...]) + jnp.log(uniform[...])
    size = jnp.max(total).astype(jnp.int32)
    which[0] = sum(jnp.where(size > NZ * (cap - 2), 1, 0) for cap in BLOCKS[:-1])


def kernel(
    cap, vec, own, head, out_v, out_l, out_e,
    w, hid, comp, acc, pick, tok, pp, reach, rq, rs, sq, ss,
    scores, tpk, send_a, recv_a, send_b, recv_b, ext,
    loc, gs, gr, pr, qs, qr, ps, pq, a_s, a_r, b_s, b_r, e_s, e_r,
):
    rows = cap * NZ
    nodes = tok.shape[1]
    groups = nodes // 128
    width = head.shape[1]
    part = hid.shape[2]
    tiles = width // TILE
    x, y = lax.axis_index("gx_0"), lax.axis_index("gx_1")
    c, z = lax.axis_index("gx_2"), lax.axis_index("gy")
    gx = (x * NY + y) * NC + c
    first = c == 0

    load_w = pltpu.make_async_copy(head, w, loc.at[2])
    load_w.start()
    own_rows = pl.ds(pl.multiple_of(gx * 2 * HALF, 2 * HALF), 2 * HALF)
    loads = [
        pltpu.make_async_copy(own.at[:, pl.ds(k * part, part)], hid.at[k, own_rows], loc.at[k])
        for k in range(2)
    ]
    for load in loads:
        load.start()

    xs = [lax.rem(x + d, NX) for d in range(NX)]
    ys = [lax.rem(y + d, NY) for d in range(NY)]
    peers = []
    for dx in (2, 1, 3, 0):
        for dy in (2, 1, 3, 0):
            for other in (1, 0):
                if dx or dy or other:
                    core = 1 - c if other else c
                    peers.append(((xs[dx] * NY + ys[dy]) * NC + core, (xs[dx], ys[dy], core, z)))
    stack = [(p, (x, y, c, p)) for p in (lax.rem(z + d, NZ) for d in (4, 3, 5, 2, 6, 1, 7))]

    barrier = pltpu.get_barrier_semaphore()
    for _, to in peers + stack:
        pl.semaphore_signal(barrier, inc=1, device_id=to, device_id_type=AT)
    for load in loads:
        load.wait()
    pl.semaphore_wait(barrier, len(peers) + len(stack))

    places = {}

    def block(da, db, h, core):
        straight = core == 0
        bx = lax.rem(x + jnp.where(straight, da, db), NX)
        by = lax.rem(y + jnp.where(straight, db, da), NY)
        at = (((bx * NY + by) * NC + core) * 2 + h) * HALF
        return pl.ds(pl.multiple_of(at, HALF), HALF)

    for da in range(4):
        for db in range(4):
            for h in range(2):
                places[da, db, h] = block(da, db, h, c)

    sent = []
    counts = {}

    def chip(axis, step):
        along_x = first if axis == 0 else jnp.logical_not(first)
        tx = lax.rem(x + jnp.where(along_x, step, 0) + NX, NX)
        ty = lax.rem(y + jnp.where(along_x, 0, step) + NY, NY)
        return (tx, ty, c, z)

    chips = {(axis, step): chip(axis, step) for axis in range(2) for step in (1, -1)}
    partner = (x, y, 1 - c, z)

    def push(k, da, db, h, arrival, to):
        here = hid.at[k, places[da, db, h]]
        n = counts.get((k, h), 0)
        counts[k, h] = n + 1
        copy = pltpu.make_async_remote_copy(
            src_ref=here, dst_ref=here, send_sem=gs.at[k, h, n], recv_sem=arrival,
            device_id=to, device_id_type=AT,
        )
        copy.start()
        sent.append(copy)

    def send(k, da, db, h, axis, step):
        ra = (da - step) % 4 if axis == 0 else da
        rb = (db - step) % 4 if axis == 1 else db
        push(k, da, db, h, gr.at[k, h, ra, rb], chips[axis, step])

    def share(k, da, db, h):
        push(k, da, db, h, pr.at[k, h, da, db], partner)

    def landed(ref, arrival):
        pltpu.make_async_remote_copy(
            src_ref=ref, dst_ref=ref, send_sem=gs.at[0, 0, 0], recv_sem=arrival,
            device_id=partner, device_id_type=AT,
        ).wait_recv()

    def arrive(k, da, db, h):
        landed(hid.at[k, places[da, db, h]], gr.at[k, h, da, db])

    def arrive_partner(k):
        for h in range(2):
            for da in range(4):
                for db in range(4):
                    landed(hid.at[k, block(da, db, h, 1 - c)], pr.at[k, h, da, db])

    sign = (1, -1)

    def level_0(k):
        for h in range(2):
            for axis in range(2):
                for step in (1, -1):
                    send(k, 0, 0, h, axis, step)
        for h in range(2):
            share(k, 0, 0, h)

    def level_1(k):
        for h in range(2):
            s = sign[h]
            for da, db in ((-s % 4, 0), (s % 4, 0), (0, -s % 4), (0, s % 4)):
                arrive(k, da, db, h)
                if db == 0:
                    if da == -s % 4:
                        send(k, da, db, h, 0, s)
                    send(k, da, db, h, 1, 1)
                    send(k, da, db, h, 1, -1)
                elif db == -s % 4:
                    send(k, da, db, h, 1, s)
                share(k, da, db, h)

    def level_2(k):
        for h in range(2):
            s = sign[h]
            arrive(k, 2, 0, h)
            send(k, 2, 0, h, 1, 1)
            send(k, 2, 0, h, 1, -1)
            share(k, 2, 0, h)
            for db in (-s % 4, s % 4):
                for da in (3, 1):
                    arrive(k, da, db, h)
                    if db == -s % 4:
                        send(k, da, db, h, 1, s)
                    share(k, da, db, h)
            arrive(k, 0, 2, h)
            share(k, 0, 2, h)

    def level_3(k):
        for h in range(2):
            s = sign[h]
            for db in (-s % 4, s % 4):
                arrive(k, 2, db, h)
                if db == -s % 4:
                    send(k, 2, db, h, 1, s)
                share(k, 2, db, h)
            for da in (3, 1):
                arrive(k, da, 2, h)
                share(k, da, 2, h)

    def level_4(k):
        for h in range(2):
            arrive(k, 2, 2, h)
            share(k, 2, 2, h)

    level_0(0)
    level_0(1)

    per = cap - 2
    order = vec[56:64, :]
    home = jnp.zeros_like(order)
    for i in range(1, NZ):
        home = home + (order >= float(i * per)).astype(F32)
    spot = home * cap + (order - home * per) + 2.0
    ends = vec[24:32, :]
    pair = jnp.floor(ends * 0.5)
    end_spot = jnp.where(ends >= 0.0, pair * cap + (ends - 2.0 * pair), -1.0)
    pos = jnp.where(vec[16:24, :] > 0.0, spot, end_spot)
    pos_id = pos.astype(jnp.int32)

    def mark(j, _):
        at = pl.ds(pl.multiple_of(j * 128, 128), 128)
        for t in range(groups):
            same = iota((128, 128), 0) + j * 128 == pos_id[t : t + 1, :]
            pick[at, t * 128 : (t + 1) * 128] = same.astype(F32).astype(BF16)
        return 0

    lax.fori_loop(0, rows // 128, mark, 0)
    level_1(0)
    level_1(1)

    token = vec[8:16, :].astype(jnp.int32) - gx * width

    def token_rows(j, _):
        at = pl.ds(pl.multiple_of(j * 128, 128), 128)
        for t in range(groups):
            same = iota((128, 128), 0) + j * 128 == token[t : t + 1, :]
            tok[at, t * 128 : (t + 1) * 128] = same.astype(F32).astype(BF16)
        return 0

    lax.fori_loop(0, width // 128, token_rows, 0)
    level_2(0)
    level_2(1)
    upper = jnp.floor(pos * (1.0 / 32.0))
    lower = pos - 32.0 * upper
    parents = vec[0:8, :].astype(jnp.int32)
    for t in range(groups):
        hit = (iota((128, 128), 0) == parents[t : t + 1, :]).astype(F32).astype(BF16)
        both = two_rows(upper[t : t + 1, :], lower[t : t + 1, :])
        got = jnp.dot(both, hit, preferred_element_type=F32)
        pp[t : t + 1, :] = got[0:1, :] * 32.0 + got[1:2, :]
    group = gx // 4
    up = vec[pl.ds(group, 1), :].astype(jnp.int32)
    line, lane_ids = iota((128, 128), 0), iota((128, 128), 1)
    reach[...] = jnp.where(line == up, 1.0, jnp.where(line == lane_ids, 1.0, 0.0))

    level_3(0)
    level_3(1)

    def spread(_, carry):
        now = reach[...].astype(BF16)
        reach[...] = jnp.minimum(jnp.dot(now, now, preferred_element_type=F32), 1.0)
        return carry

    lax.fori_loop(0, 6, spread, 0)
    level_4(0)

    def select(k):
        def body(j, _):
            lane = pl.ds(pl.multiple_of(j * TILE, TILE), TILE)
            comp[k, :, lane] = jnp.dot(
                pick[...], hid[k, :, lane], preferred_element_type=F32
            ).astype(BF16)
            return 0

        lax.fori_loop(0, part // TILE, body, 0)

    arrive_partner(0)
    select(0)
    level_4(1)
    load_w.wait()

    def lanes_of(j):
        return pl.ds(pl.multiple_of(j * TILE, TILE), TILE)

    def quantize(v, m, j):
        top = jnp.maximum(jnp.max(jnp.abs(v), axis=0, keepdims=True), 1e-30)
        ss[m, j] = top * (1.0 / 32767.0)
        sq[m, j] = jnp.round(v * (32767.0 / top)).astype(jnp.int32).astype(jnp.int16)

    above, below = (x, y, c, lax.rem(z + 1, NZ)), (x, y, c, lax.rem(z + NZ - 1, NZ))

    def ring_copies(m, j, way):
        to = above if (way == 0) == (m < LONG) else below
        return (
            pltpu.make_async_remote_copy(
                src_ref=sq.at[m, j], dst_ref=rq.at[m, j], send_sem=qs.at[m, j],
                recv_sem=qr.at[m, j], device_id=to, device_id_type=AT),
            pltpu.make_async_remote_copy(
                src_ref=ss.at[m, j], dst_ref=rs.at[m, j], send_sem=ps.at[m, j],
                recv_sem=pq.at[m, j], device_id=to, device_id_type=AT),
        )

    def rows_of(steps):
        d = lax.rem(z + steps + NZ, NZ)
        return pl.ds(pl.multiple_of(d * cap, 16), cap)

    def goal(m, way):
        s = 1 if way == 0 else -1
        return s * (LONG - m) if m < LONG else -s * (NZ - 1 - m)

    def forward(v, m, j, way):
        quantize(v, m, j)
        for copy in ring_copies(m, j, way):
            copy.start()

    def arrived(m, j, way):
        for copy in ring_copies(m, j, way):
            copy.wait_recv()
        return rq[m, j].astype(jnp.int32).astype(F32) * rs[m, j]

    def lower_half(j, _):
        acc[:, lanes_of(j)] = jnp.dot(comp[0], w[0:part, lanes_of(j)], preferred_element_type=F32)
        return 0

    lax.fori_loop(0, tiles, lower_half, 0)
    arrive_partner(1)
    select(1)

    def upper_half(jj, _):
        for way in range(2):
            j = jj * 2 + way
            acc[:, lanes_of(j)] += jnp.dot(
                comp[1], w[part : 2 * part, lanes_of(j)], preferred_element_type=F32
            )
            for m in (0, LONG):
                forward(acc[rows_of(goal(m, way)), lanes_of(j)], m, j, way)
        return 0

    lax.fori_loop(0, tiles // 2, upper_half, 0)

    for hop in range(1, LONG):
        def pass_on(jj, _, hop=hop):
            for way in range(2):
                j = jj * 2 + way
                for m in (hop, LONG + hop):
                    if m < NZ - 1:
                        got = arrived(m - 1, j, way)
                        forward(got + acc[rows_of(goal(m, way)), lanes_of(j)], m, j, way)
            return 0

        lax.fori_loop(0, tiles // 2, pass_on, 0)

    tpk[...] = jnp.zeros_like(tpk)

    def finish(jj, _):
        for way in range(2):
            j = jj * 2 + way
            v = acc[rows_of(0), lanes_of(j)] + arrived(NZ - 2, j, way) + arrived(LONG - 1, j, way)
            scores[:, lanes_of(j)] = v
            high = v.astype(BF16)
            rest = v - high.astype(F32)
            middle = rest.astype(BF16)
            low = (rest - middle.astype(F32)).astype(BF16)
            got = jnp.dot(
                jnp.concatenate([high, middle, low], axis=0), tok[lanes_of(j), :],
                preferred_element_type=F32,
            )
            tpk[...] += got[0:cap] + got[cap : 2 * cap] + got[2 * cap : 3 * cap]
        return 0

    lax.fori_loop(0, tiles // 2, finish, 0)

    ext[z] = scores[0:2, :]
    ext_copies = [
        pltpu.make_async_remote_copy(
            src_ref=ext.at[z], dst_ref=ext.at[z], send_sem=e_s.at[k],
            recv_sem=e_r.at[z], device_id=to, device_id_type=AT)
        for k, (_, to) in enumerate(stack)
    ]
    for copy in ext_copies:
        copy.start()

    top = jnp.max(scores[...], axis=1, keepdims=True)
    total = jnp.sum(jnp.exp(scores[...] - top), axis=1, keepdims=True)
    top_row, total_row = to_row(top, 128), to_row(total, 128)
    base = (z * cap).astype(F32)
    places_here = iota((cap, 128), 0).astype(F32) + base
    for t in range(groups):
        held = places_here == pp[t : t + 1, :]
        target = jnp.sum(
            jnp.where(held, tpk[:, t * 128 : (t + 1) * 128], 0.0), axis=0, keepdims=True
        )
        send_a[t] = jnp.concatenate([target, top_row, total_row], axis=1)
    recv_a[gx] = send_a[group]
    plane_copies = [
        pltpu.make_async_remote_copy(
            src_ref=send_a.at[p // 4], dst_ref=recv_a.at[gx], send_sem=a_s.at[k],
            recv_sem=a_r.at[gx], device_id=to, device_id_type=AT)
        for k, (p, to) in enumerate(peers)
    ]
    for copy in plane_copies:
        copy.start()

    for copy in sent:
        copy.wait_send()

    def ring_drain(jj, _):
        for way in range(2):
            for m in range(NZ - 1):
                for copy in ring_copies(m, jj * 2 + way, way):
                    copy.wait_send()
        return 0

    lax.fori_loop(0, tiles // 2, ring_drain, 0)
    for k, (p, to) in enumerate(reversed(peers)):
        landed(recv_a.at[p], a_r.at[p])
    parts = [recv_a[k] for k in range(PLANE)]
    tops = [p[:, 128:256] for p in parts]
    while len(tops) > 1:
        tops = [jnp.maximum(a, b) for a, b in zip(tops[::2], tops[1::2])]
    sums = [p[:, 256:384] * jnp.exp(p[:, 128:256] - tops[0]) for p in parts]
    wanted = [p[:, 0:128] for p in parts]
    while len(sums) > 1:
        sums = [a + b for a, b in zip(sums[::2], sums[1::2])]
        wanted = [a + b for a, b in zip(wanted[::2], wanted[1::2])]
    used = iota((1, 128), 1) < cap
    log_total = jnp.where(used, tops[0] + jnp.log(jnp.where(used, sums[0], 1.0)), 0.0)
    column = to_column(log_total, cap)
    here = places_here == pp[pl.ds(group, 1), :]
    mine_part = wanted[0] - jnp.sum(jnp.where(here, column, 0.0), axis=0, keepdims=True)
    send_b[...] = jnp.concatenate([mine_part, log_total], axis=1)
    recv_b[z] = send_b[...]
    b_copies = [
        pltpu.make_async_remote_copy(
            src_ref=send_b, dst_ref=recv_b.at[z], send_sem=b_s.at[k],
            recv_sem=b_r.at[z], device_id=to, device_id_type=AT)
        for k, (_, to) in enumerate(stack)
    ]
    for copy in b_copies:
        copy.start()
    for copy in plane_copies + ext_copies:
        copy.wait_send()
    for p, _ in stack:
        landed(ext.at[p], e_r.at[p])
    for p, _ in reversed(stack):
        landed(recv_b.at[p], b_r.at[p])

    margin = recv_b[0][:, 0:128]
    for k in range(1, NZ):
        margin = margin + recv_b[k][:, 0:128]
    margin = margin - vec[pl.ds(48 + group, 1), :]
    spare = vec[pl.ds(32 + group, 1), :] > 0.0
    climb = to_column(jnp.where(vec[pl.ds(40 + group, 1), :] > 0.0, BIG, margin), 128)
    least = jnp.min(jnp.where(reach[...] > 0.0, climb, BIG), axis=0, keepdims=True)
    both = jnp.where(
        iota((8, 128), 0) == 0,
        jnp.where(spare, 0.0, margin),
        jnp.where(spare, 0.0, least),
    )
    both = pltpu.roll(both, lax.rem(128 - 2 * HALF * lax.rem(gx, 4), 128), axis=1)
    out_v[...] = both[0:1, 0 : 2 * HALF]
    out_l[...] = both[1:2, 0 : 2 * HALF]
    lane = iota((1, 128), 1)
    for k in range(NZ):
        line = recv_b[k][:, 128:256]
        low = jnp.sum(jnp.where(lane == 0, line, 0.0), axis=1, keepdims=True)
        high = jnp.sum(jnp.where(lane == 1, line, 0.0), axis=1, keepdims=True)
        out_e[2 * k : 2 * k + 2, :] = ext[k] - jnp.where(iota((2, 1), 0) == 0, low, high)
    for copy in b_copies:
        copy.wait_send()


def fused(cap, number, vec, hidden, head):
    depth, width = head.shape
    nodes = hidden.shape[0] * PLANE
    rows, tiles, hops = cap * NZ, width // TILE, NZ - 1
    dma = pltpu.SemaphoreType.DMA
    vmem = pl.BlockSpec(memory_space=pltpu.VMEM)
    far = pl.BlockSpec(memory_space=pl.ANY)
    return pl.pallas_call(
        functools.partial(kernel, cap),
        out_shape=(
            jax.ShapeDtypeStruct((1, 2 * HALF), F32),
            jax.ShapeDtypeStruct((1, 2 * HALF), F32),
            jax.ShapeDtypeStruct((2 * NZ, width), F32),
        ),
        in_specs=[vmem, far, far],
        out_specs=(vmem, vmem, vmem),
        scratch_shapes=[
            pltpu.VMEM((depth, width), BF16),
            pltpu.VMEM((2, nodes, depth // 2), BF16),
            pltpu.VMEM((2, rows, depth // 2), BF16),
            pltpu.VMEM((rows, width), F32),
            pltpu.VMEM((rows, nodes), BF16),
            pltpu.VMEM((width, nodes), BF16),
            pltpu.VMEM((8, 128), F32),
            pltpu.VMEM((128, 128), F32),
            pltpu.VMEM((hops, tiles, cap, TILE), jnp.int16),
            pltpu.VMEM((hops, tiles, 1, TILE), F32),
            pltpu.VMEM((hops, tiles, cap, TILE), jnp.int16),
            pltpu.VMEM((hops, tiles, 1, TILE), F32),
            pltpu.VMEM((cap, width), F32),
            pltpu.VMEM((cap, nodes), F32),
            pltpu.VMEM((nodes // 128, 1, 384), F32),
            pltpu.VMEM((PLANE, 1, 384), F32),
            pltpu.VMEM((1, 256), F32),
            pltpu.VMEM((NZ, 1, 256), F32),
            pltpu.VMEM((NZ, 2, width), F32),
            dma((3,)),
            dma((2, 2, 31)),
            dma((2, 2, 4, 4)),
            dma((2, 2, 4, 4)),
            dma((hops, tiles)),
            dma((hops, tiles)),
            dma((hops, tiles)),
            dma((hops, tiles)),
            dma((PLANE,)),
            dma((PLANE,)),
            dma((NZ,)),
            dma((NZ,)),
            dma((NZ,)),
            dma((NZ,)),
        ],
        compiler_params=pltpu.CompilerParams(
            collective_id=number, has_side_effects=True, vmem_limit_bytes=67043328
        ),
        name=f"head_{cap}",
    )(vec, hidden, head)


def local(hidden, lm_head, parent, draft_token, draft_prob, uniforms, node_count, accepted_end):
    lines = (parent.shape[0] // 128, 128)
    vmem, smem = pl.BlockSpec(memory_space=pltpu.VMEM), pl.BlockSpec(memory_space=pltpu.SMEM)
    vec, which = pl.pallas_call(
        plan,
        out_shape=(
            jax.ShapeDtypeStruct((64, 128), F32),
            jax.ShapeDtypeStruct((1,), jnp.int32),
        ),
        in_specs=[vmem, smem, smem, vmem, vmem, vmem],
        out_specs=(vmem, smem),
        name="plan",
    )(
        parent.reshape(lines), node_count, accepted_end, draft_token.reshape(lines),
        draft_prob.reshape(lines), uniforms.reshape(lines),
    )
    branches = [functools.partial(fused, cap, i) for i, cap in enumerate(BLOCKS)]
    slack, least, extra = lax.switch(which[0], branches, vec, hidden, lm_head)
    return slack.reshape(-1), least.reshape(-1), extra


def solution(mesh):
    finer = Mesh(mesh.devices.reshape(NX, NY, NC, NZ), ALL)
    placed = (P(GX, "gy"), P("gy", GX), P(), P(), P(), P(), P(), P())
    return jax.shard_map(
        local, mesh=finer, in_specs=placed, out_specs=(P(GX), P(GX), P(None, GX)), check_vma=False
    )
```

```python
import functools

import jax
import jax.numpy as jnp
from jax import lax
from jax.experimental import pallas as pl
from jax.experimental.pallas import tpu as pltpu
from jax.sharding import Mesh
from jax.sharding import PartitionSpec as P

GX = ("gx_0", "gx_1", "gx_2")
ALL = ("gx_0", "gx_1", "gx_2", "gy")
NX, NY, NC, NZ = 4, 4, 2, 8
PLANE = NX * NY * NC
HALF = 16
TILE = 512
LONG = 4
BLOCKS = (40, 48, 56, 64, 128)
BIG = 10000.0
F32 = jnp.float32
BF16 = jnp.bfloat16
AT = pl.DeviceIdType.MESH


def iota(shape, dim):
    return lax.broadcasted_iota(jnp.int32, shape, dim)


def to_column(row, rows):
    spread = jnp.broadcast_to(row, (rows, row.shape[1]))
    keep = iota(spread.shape, 0) == iota(spread.shape, 1)
    return jnp.sum(jnp.where(keep, spread, 0.0), axis=1, keepdims=True)


def to_row(column, lanes):
    spread = jnp.broadcast_to(column, (column.shape[0], lanes))
    keep = iota(spread.shape, 0) == iota(spread.shape, 1)
    return jnp.sum(jnp.where(keep, spread, 0.0), axis=0, keepdims=True)


def two_rows(first, second):
    lines = iota((16, first.shape[1]), 0)
    return jnp.where(lines == 0, first, jnp.where(lines == 1, second, 0.0)).astype(BF16)


def plan(parent, counts, ends, token, prob, uniform, vec, which):
    shape = parent.shape
    lines, lanes = iota((1, 128), 0), iota((1, 128), 1)
    total = jnp.zeros((1, 128), F32)
    before = (iota((128, 128), 0) < iota((128, 128), 1)).astype(F32).astype(BF16)
    order, reads = [], []
    for t in range(shape[0]):
        second = lanes >= 64
        slot = jnp.where(second, lanes - 64, lanes)
        live = slot < jnp.where(second, counts[2 * t + 1], counts[2 * t])
        end = slot == jnp.where(second, ends[2 * t + 1], ends[2 * t])
        up = parent[t : t + 1, :] - t * 128
        root = up == lanes
        child = jnp.where(live & jnp.logical_not(root), up.astype(F32), -1.0)
        column = to_column(child, 128)
        hit = (column == iota((128, 128), 1).astype(F32)).astype(F32)
        needed = jnp.max(hit, axis=0, keepdims=True)
        plain = jnp.where(end, 0.0, needed)
        vec[0 + t : 1 + t, :] = up.astype(F32)
        vec[16 + t : 17 + t, :] = plain
        vec[24 + t : 25 + t, :] = jnp.where(end, jnp.where(second, 2 * t + 1, 2 * t), -1).astype(F32)
        vec[32 + t : 33 + t, :] = jnp.where(root, 1.0, jnp.where(live, 0.0, 1.0))
        vec[40 + t : 41 + t, :] = root.astype(F32)
        within = jnp.dot(
            jnp.broadcast_to(plain, (16, 128)).astype(BF16), before, preferred_element_type=F32
        )[0:1, :]
        vec[56 + t : 57 + t, :] = within + total
        total = total + jnp.sum(plain, axis=1, keepdims=True)
    vec[8:16, :] = token[...].astype(F32)
    vec[48:56, :] = jnp.log(prob[...]) + jnp.log(uniform[...])
    size = jnp.max(total).astype(jnp.int32)
    which[0] = sum(jnp.where(size > NZ * (cap - 2), 1, 0) for cap in BLOCKS[:-1])


def kernel(
    cap, vec, own, head, out_s, out_e,
    w, hid, comp, acc, pick, tok, pp, reach, rq, rs, sq, ss,
    scores, tpk, send_a, recv_a, send_b, recv_b, ext,
    loc, gs, gr, pr, qs, qr, ps, pq, a_s, a_r, b_s, b_r, e_s, e_r,
):
    rows = cap * NZ
    nodes = tok.shape[1]
    groups = nodes // 128
    width = head.shape[1]
    tiles = width // TILE
    x, y = lax.axis_index("gx_0"), lax.axis_index("gx_1")
    c, z = lax.axis_index("gx_2"), lax.axis_index("gy")
    gx = (x * NY + y) * NC + c
    first = c == 0

    load_w = pltpu.make_async_copy(head, w, loc.at[1])
    load_w.start()
    own_rows = pl.ds(pl.multiple_of(gx * 2 * HALF, 2 * HALF), 2 * HALF)
    load_own = pltpu.make_async_copy(own, hid.at[own_rows], loc.at[0])
    load_own.start()

    xs = [lax.rem(x + d, NX) for d in range(NX)]
    ys = [lax.rem(y + d, NY) for d in range(NY)]
    peers = []
    for dx in (2, 1, 3, 0):
        for dy in (2, 1, 3, 0):
            for other in (1, 0):
                if dx or dy or other:
                    core = 1 - c if other else c
                    peers.append(((xs[dx] * NY + ys[dy]) * NC + core, (xs[dx], ys[dy], core, z)))
    stack = [(p, (x, y, c, p)) for p in (lax.rem(z + d, NZ) for d in (4, 3, 5, 2, 6, 1, 7))]

    barrier = pltpu.get_barrier_semaphore()
    for _, to in peers + stack:
        pl.semaphore_signal(barrier, inc=1, device_id=to, device_id_type=AT)
    load_own.wait()
    pl.semaphore_wait(barrier, len(peers) + len(stack))

    places = {}

    def block(da, db, h, core):
        straight = core == 0
        bx = lax.rem(x + jnp.where(straight, da, db), NX)
        by = lax.rem(y + jnp.where(straight, db, da), NY)
        at = (((bx * NY + by) * NC + core) * 2 + h) * HALF
        return pl.ds(pl.multiple_of(at, HALF), HALF)

    for da in range(4):
        for db in range(4):
            for h in range(2):
                places[da, db, h] = block(da, db, h, c)

    sent = []
    counts = {}

    def chip(axis, step):
        along_x = first if axis == 0 else jnp.logical_not(first)
        tx = lax.rem(x + jnp.where(along_x, step, 0) + NX, NX)
        ty = lax.rem(y + jnp.where(along_x, 0, step) + NY, NY)
        return (tx, ty, c, z)

    chips = {(axis, step): chip(axis, step) for axis in range(2) for step in (1, -1, 2)}
    partner = (x, y, 1 - c, z)

    def push(da, db, h, arrival, to):
        here = hid.at[places[da, db, h]]
        n = counts.get(h, 0)
        counts[h] = n + 1
        copy = pltpu.make_async_remote_copy(
            src_ref=here, dst_ref=here, send_sem=gs.at[h, n], recv_sem=arrival,
            device_id=to, device_id_type=AT,
        )
        copy.start()
        sent.append(copy)

    def send(da, db, h, axis, step):
        ra = (da - step) % 4 if axis == 0 else da
        rb = (db - step) % 4 if axis == 1 else db
        push(da, db, h, gr.at[h, ra, rb], chips[axis, step])

    def share(da, db, h):
        push(da, db, h, pr.at[h, da, db], partner)

    def landed(ref, arrival):
        pltpu.make_async_remote_copy(
            src_ref=ref, dst_ref=ref, send_sem=gs.at[0, 0], recv_sem=arrival,
            device_id=partner, device_id_type=AT,
        ).wait_recv()

    def arrive(da, db, h):
        landed(hid.at[places[da, db, h]], gr.at[h, da, db])

    def arrive_partner(dx):
        for h in range(2):
            for k in range(4):
                da, db = jnp.where(first, k, dx), jnp.where(first, dx, k)
                landed(hid.at[block(da, db, h, 1 - c)], pr.at[h, da, db])

    sign = (1, -1)
    away = (2, 3, 1)

    def level_0():
        for h in range(2):
            for step in (2, 1, -1):
                send(0, 0, h, 0, step)
            for step in (1, -1):
                send(0, 0, h, 1, step)
        for h in range(2):
            share(0, 0, h)

    def level_1():
        for h in range(2):
            s = sign[h]
            for da in (s % 4, -s % 4, 2):
                arrive(da, 0, h)
                send(da, 0, h, 1, s)
                send(da, 0, h, 1, -s)
            arrive(0, -s % 4, h)
            send(0, -s % 4, h, 1, s)
            arrive(0, s % 4, h)
        for h in range(2):
            for da in away:
                share(da, 0, h)
            for db in (3, 1):
                share(0, db, h)

    def level_2():
        for h in range(2):
            s = sign[h]
            for da in (3, 1, 2):
                arrive(da, -s % 4, h)
                send(da, -s % 4, h, 1, s)
        for h in range(2):
            s = sign[h]
            arrive(0, 2, h)
            share(0, 2, h)
            for da in (3, 1, 2):
                share(da, -s % 4, h)
                arrive(da, s % 4, h)
                share(da, s % 4, h)

    def level_3():
        for da in (3, 1, 2):
            for h in range(2):
                arrive(da, 2, h)
                share(da, 2, h)

    level_0()

    per = cap - 2
    order = vec[56:64, :]
    home = jnp.zeros_like(order)
    for i in range(1, NZ):
        home = home + (order >= float(i * per)).astype(F32)
    spot = home * cap + (order - home * per) + 2.0
    ends = vec[24:32, :]
    pair = jnp.floor(ends * 0.5)
    end_spot = jnp.where(ends >= 0.0, pair * cap + (ends - 2.0 * pair), -1.0)
    pos = jnp.where(vec[16:24, :] > 0.0, spot, end_spot)
    pos_id = pos.astype(jnp.int32)

    def mark(j, _):
        at = pl.ds(pl.multiple_of(j * 64, 64), 64)
        for t in range(groups):
            same = iota((64, 128), 0) + j * 64 == pos_id[t : t + 1, :]
            pick[at, t * 128 : (t + 1) * 128] = same.astype(F32).astype(BF16)
        return 0

    lax.fori_loop(0, rows // 64, mark, 0)
    level_1()

    token = vec[8:16, :].astype(jnp.int32) - gx * width

    def token_rows(j, _):
        at = pl.ds(pl.multiple_of(j * 128, 128), 128)
        for t in range(groups):
            same = iota((128, 128), 0) + j * 128 == token[t : t + 1, :]
            tok[at, t * 128 : (t + 1) * 128] = same.astype(F32).astype(BF16)
        return 0

    lax.fori_loop(0, width // 128, token_rows, 0)
    upper = jnp.floor(pos * (1.0 / 32.0))
    lower = pos - 32.0 * upper
    parents = vec[0:8, :].astype(jnp.int32)
    for t in range(groups):
        hit = (iota((128, 128), 0) == parents[t : t + 1, :]).astype(F32).astype(BF16)
        both = two_rows(upper[t : t + 1, :], lower[t : t + 1, :])
        got = jnp.dot(both, hit, preferred_element_type=F32)
        pp[t : t + 1, :] = got[0:1, :] * 32.0 + got[1:2, :]
    group = gx // 4
    up = vec[pl.ds(group, 1), :].astype(jnp.int32)
    line, lane_ids = iota((128, 128), 0), iota((128, 128), 1)
    reach[...] = jnp.where(line == up, 1.0, jnp.where(line == lane_ids, 1.0, 0.0))

    level_2()

    def spread(_, carry):
        now = reach[...].astype(BF16)
        reach[...] = jnp.minimum(jnp.dot(now, now, preferred_element_type=F32), 1.0)
        return carry

    lax.fori_loop(0, 6, spread, 0)

    def select(group_of, start):
        quarter = nodes // NX
        for dx in group_of:
            arrive_partner(dx)

        def body(j, _):
            lane = pl.ds(pl.multiple_of(j * TILE, TILE), TILE)
            got = None if start else comp[:, lane].astype(F32)
            for dx in group_of:
                at = pl.ds(pl.multiple_of(xs[dx] * quarter, quarter), quarter)
                new = jnp.dot(pick[:, at], hid[at, lane], preferred_element_type=F32)
                got = new if got is None else got + new
            comp[:, lane] = got.astype(BF16)
            return 0

        lax.fori_loop(0, hid.shape[1] // TILE, body, 0)

    select((0,), True)
    level_3()
    load_w.wait()
    select((3, 1, 2), False)

    def lanes_of(j):
        return pl.ds(pl.multiple_of(j * TILE, TILE), TILE)

    def quantize(v, m, j):
        top = jnp.maximum(jnp.max(jnp.abs(v), axis=0, keepdims=True), 1e-30)
        ss[m, j] = top * (1.0 / 32767.0)
        v = jnp.round(v * (32767.0 / top))
        v = jnp.concatenate([v[:, i : i + 128] for i in range(0, TILE, 128)], axis=0)
        sq[m, j] = v.astype(jnp.int32).astype(jnp.int16)

    above, below = (x, y, c, lax.rem(z + 1, NZ)), (x, y, c, lax.rem(z + NZ - 1, NZ))

    def ring_copies(m, j, way):
        to = above if (way == 0) == (m < LONG) else below
        return (
            pltpu.make_async_remote_copy(
                src_ref=sq.at[m, j], dst_ref=rq.at[m, j], send_sem=qs.at[m, j],
                recv_sem=qr.at[m, j], device_id=to, device_id_type=AT),
            pltpu.make_async_remote_copy(
                src_ref=ss.at[m, j], dst_ref=rs.at[m, j], send_sem=ps.at[m, j],
                recv_sem=pq.at[m, j], device_id=to, device_id_type=AT),
        )

    def rows_of(steps):
        d = lax.rem(z + steps + NZ, NZ)
        return pl.ds(pl.multiple_of(d * cap, 8), cap)

    def goal(m, way):
        s = 1 if way == 0 else -1
        return s * (LONG - m) if m < LONG else -s * (NZ - 1 - m)

    def forward(v, m, j, way):
        quantize(v, m, j)
        for copy in ring_copies(m, j, way):
            copy.start()

    def arrived(m, j, way):
        for copy in ring_copies(m, j, way):
            copy.wait_recv()
        v = rq[m, j].astype(jnp.int32).astype(F32)
        v = jnp.concatenate([v[i * cap : (i + 1) * cap] for i in range(TILE // 128)], axis=1)
        return v * rs[m, j]

    def multiply(jj, _):
        for way in range(2):
            j = jj * 2 + way
            acc[:, lanes_of(j)] = jnp.dot(comp[...], w[:, lanes_of(j)], preferred_element_type=F32)
            for m in (0, LONG):
                forward(acc[rows_of(goal(m, way)), lanes_of(j)], m, j, way)
        return 0

    lax.fori_loop(0, tiles // 2, multiply, 0)

    for hop in range(1, LONG):
        def pass_on(jj, _, hop=hop):
            for way in range(2):
                j = jj * 2 + way
                for m in (hop, LONG + hop):
                    if m < NZ - 1:
                        got = arrived(m - 1, j, way)
                        forward(got + acc[rows_of(goal(m, way)), lanes_of(j)], m, j, way)
            return 0

        lax.fori_loop(0, tiles // 2, pass_on, 0)

    tpk[...] = jnp.zeros_like(tpk)

    def finish(jj, _):
        for way in range(2):
            j = jj * 2 + way
            v = acc[rows_of(0), lanes_of(j)] + arrived(NZ - 2, j, way) + arrived(LONG - 1, j, way)
            scores[:, lanes_of(j)] = v
            high = v.astype(BF16).astype(F32)
            rest = v - high
            middle = rest.astype(BF16).astype(F32)
            pieces = jnp.concatenate([high, middle, rest - middle], axis=0).astype(BF16)
            got = jnp.dot(pieces, tok[lanes_of(j), :], preferred_element_type=F32)
            tpk[...] += got[0:cap] + got[cap : 2 * cap] + got[2 * cap : 3 * cap]
        return 0

    lax.fori_loop(0, tiles // 2, finish, 0)

    ext[z] = scores[0:2, :]
    ext_copies = [
        pltpu.make_async_remote_copy(
            src_ref=ext.at[z], dst_ref=ext.at[z], send_sem=e_s.at[k],
            recv_sem=e_r.at[z], device_id=to, device_id_type=AT)
        for k, (_, to) in enumerate(stack)
    ]
    for copy in ext_copies:
        copy.start()

    top = jnp.max(scores[...], axis=1, keepdims=True)
    total = jnp.sum(jnp.exp(scores[...] - top), axis=1, keepdims=True)
    top_row, total_row = to_row(top, 128), to_row(total, 128)
    base = (z * cap).astype(F32)
    places_here = iota((cap, 128), 0).astype(F32) + base
    for t in range(groups):
        held = places_here == pp[t : t + 1, :]
        target = jnp.sum(
            jnp.where(held, tpk[:, t * 128 : (t + 1) * 128], 0.0), axis=0, keepdims=True
        )
        send_a[t] = jnp.concatenate([target, top_row, total_row], axis=1)
    recv_a[gx] = send_a[group]
    plane_copies = [
        pltpu.make_async_remote_copy(
            src_ref=send_a.at[p // 4], dst_ref=recv_a.at[gx], send_sem=a_s.at[k],
            recv_sem=a_r.at[gx], device_id=to, device_id_type=AT)
        for k, (p, to) in enumerate(peers)
    ]
    for copy in plane_copies:
        copy.start()

    for copy in sent:
        copy.wait_send()

    def ring_drain(jj, _):
        for way in range(2):
            for m in range(NZ - 1):
                for copy in ring_copies(m, jj * 2 + way, way):
                    copy.wait_send()
        return 0

    lax.fori_loop(0, tiles // 2, ring_drain, 0)
    for k, (p, to) in enumerate(reversed(peers)):
        landed(recv_a.at[p], a_r.at[p])
    parts = [recv_a[k] for k in range(PLANE)]
    tops = [p[:, 128:256] for p in parts]
    while len(tops) > 1:
        tops = [jnp.maximum(a, b) for a, b in zip(tops[::2], tops[1::2])]
    sums = [p[:, 256:384] * jnp.exp(p[:, 128:256] - tops[0]) for p in parts]
    wanted = [p[:, 0:128] for p in parts]
    while len(sums) > 1:
        sums = [a + b for a, b in zip(sums[::2], sums[1::2])]
        wanted = [a + b for a, b in zip(wanted[::2], wanted[1::2])]
    used = iota((1, 128), 1) < cap
    log_total = jnp.where(used, tops[0] + jnp.log(jnp.where(used, sums[0], 1.0)), 0.0)
    column = to_column(log_total, cap)
    here = places_here == pp[pl.ds(group, 1), :]
    mine_part = wanted[0] - jnp.sum(jnp.where(here, column, 0.0), axis=0, keepdims=True)
    send_b[...] = jnp.concatenate([mine_part, log_total], axis=1)
    recv_b[z] = send_b[...]
    b_copies = [
        pltpu.make_async_remote_copy(
            src_ref=send_b, dst_ref=recv_b.at[z], send_sem=b_s.at[k],
            recv_sem=b_r.at[z], device_id=to, device_id_type=AT)
        for k, (_, to) in enumerate(stack)
    ]
    for copy in b_copies:
        copy.start()
    for copy in plane_copies + ext_copies:
        copy.wait_send()
    for p, _ in stack:
        landed(ext.at[p], e_r.at[p])
    for p, _ in reversed(stack):
        landed(recv_b.at[p], b_r.at[p])

    margin = recv_b[0][:, 0:128]
    for k in range(1, NZ):
        margin = margin + recv_b[k][:, 0:128]
    margin = margin - vec[pl.ds(48 + group, 1), :]
    spare = vec[pl.ds(32 + group, 1), :] > 0.0
    climb = to_column(jnp.where(vec[pl.ds(40 + group, 1), :] > 0.0, BIG, margin), 128)
    least = jnp.min(jnp.where(reach[...] > 0.0, climb, BIG), axis=0, keepdims=True)
    both = jnp.where(
        iota((8, 128), 0) == 0,
        jnp.where(spare, 0.0, margin),
        jnp.where(spare, 0.0, least),
    )
    both = pltpu.roll(both, lax.rem(128 - 2 * HALF * lax.rem(gx, 4), 128), axis=1)
    out_s[...] = both
    lane = iota((1, 128), 1)
    for k in range(NZ):
        line = recv_b[k][:, 128:256]
        low = jnp.sum(jnp.where(lane == 0, line, 0.0), axis=1, keepdims=True)
        high = jnp.sum(jnp.where(lane == 1, line, 0.0), axis=1, keepdims=True)
        out_e[2 * k : 2 * k + 2, :] = ext[k] - jnp.where(iota((2, 1), 0) == 0, low, high)
    for copy in b_copies:
        copy.wait_send()


def fused(cap, number, vec, hidden, head):
    depth, width = head.shape
    nodes = hidden.shape[0] * PLANE
    rows, tiles, hops = cap * NZ, width // TILE, NZ - 1
    dma = pltpu.SemaphoreType.DMA
    vmem = pl.BlockSpec(memory_space=pltpu.VMEM)
    far = pl.BlockSpec(memory_space=pl.ANY)
    return pl.pallas_call(
        functools.partial(kernel, cap),
        out_shape=(
            jax.ShapeDtypeStruct((8, 128), F32),
            jax.ShapeDtypeStruct((2 * NZ, width), F32),
        ),
        in_specs=[vmem, far, far],
        out_specs=(vmem, vmem),
        scratch_shapes=[
            pltpu.VMEM((depth, width), BF16),
            pltpu.VMEM((nodes, depth), BF16),
            pltpu.VMEM((rows, depth), BF16),
            pltpu.VMEM((rows, width), F32),
            pltpu.VMEM((rows, nodes), BF16),
            pltpu.VMEM((width, nodes), BF16),
            pltpu.VMEM((8, 128), F32),
            pltpu.VMEM((128, 128), F32),
            pltpu.VMEM((hops, tiles, TILE // 128 * cap, 128), jnp.int16),
            pltpu.VMEM((hops, tiles, 1, TILE), F32),
            pltpu.VMEM((hops, tiles, TILE // 128 * cap, 128), jnp.int16),
            pltpu.VMEM((hops, tiles, 1, TILE), F32),
            pltpu.VMEM((cap, width), F32),
            pltpu.VMEM((cap, nodes), F32),
            pltpu.VMEM((nodes // 128, 1, 384), F32),
            pltpu.VMEM((PLANE, 1, 384), F32),
            pltpu.VMEM((1, 256), F32),
            pltpu.VMEM((NZ, 1, 256), F32),
            pltpu.VMEM((NZ, 2, width), F32),
            dma((2,)),
            dma((2, 31)),
            dma((2, 4, 4)),
            dma((2, 4, 4)),
            dma((hops, tiles)),
            dma((hops, tiles)),
            dma((hops, tiles)),
            dma((hops, tiles)),
            dma((PLANE,)),
            dma((PLANE,)),
            dma((NZ,)),
            dma((NZ,)),
            dma((NZ,)),
            dma((NZ,)),
        ],
        compiler_params=pltpu.CompilerParams(
            collective_id=number, has_side_effects=True, vmem_limit_bytes=67043328
        ),
        name=f"head_{cap}",
    )(vec, hidden, head)


def local(hidden, lm_head, parent, draft_token, draft_prob, uniforms, node_count, accepted_end):
    lines = (parent.shape[0] // 128, 128)
    vmem, smem = pl.BlockSpec(memory_space=pltpu.VMEM), pl.BlockSpec(memory_space=pltpu.SMEM)
    vec, which = pl.pallas_call(
        plan,
        out_shape=(
            jax.ShapeDtypeStruct((64, 128), F32),
            jax.ShapeDtypeStruct((1,), jnp.int32),
        ),
        in_specs=[vmem, smem, smem, vmem, vmem, vmem],
        out_specs=(vmem, smem),
        name="plan",
    )(
        parent.reshape(lines), node_count, accepted_end, draft_token.reshape(lines),
        draft_prob.reshape(lines), uniforms.reshape(lines),
    )

    def branch(i, *args):
        small, extra = fused(BLOCKS[i], i, *args)
        return small[0, : 2 * HALF], small[1, : 2 * HALF], extra

    branches = [functools.partial(branch, i) for i in range(len(BLOCKS))]
    return lax.switch(which[0], branches, vec, hidden, lm_head)


def solution(mesh):
    finer = Mesh(mesh.devices.reshape(NX, NY, NC, NZ), ALL)
    placed = (P(GX, "gy"), P("gy", GX), P(), P(), P(), P(), P(), P())
    return jax.shard_map(
        local, mesh=finer, in_specs=placed, out_specs=(P(GX), P(GX), P(None, GX)), check_vma=False
    )
```

```python
import functools

import jax
import jax.numpy as jnp
from jax import lax
from jax.experimental import pallas as pl
from jax.experimental.pallas import tpu as pltpu
from jax.sharding import Mesh
from jax.sharding import PartitionSpec as P

GX = ("gx_0", "gx_1", "gx_2")
ALL = ("gx_0", "gx_1", "gx_2", "gy")
NX, NY, NC, NZ = 4, 4, 2, 8
PLANE = NX * NY * NC
HALF = 16
TILE = 512
LONG = 4
BLOCKS = (40, 48, 56, 64, 128)
BIG = 10000.0
F32 = jnp.float32
BF16 = jnp.bfloat16
AT = pl.DeviceIdType.MESH


def iota(shape, dim):
    return lax.broadcasted_iota(jnp.int32, shape, dim)


def to_column(row, rows):
    spread = jnp.broadcast_to(row, (rows, row.shape[1]))
    keep = iota(spread.shape, 0) == iota(spread.shape, 1)
    return jnp.sum(jnp.where(keep, spread, 0.0), axis=1, keepdims=True)


def to_row(column, lanes):
    spread = jnp.broadcast_to(column, (column.shape[0], lanes))
    keep = iota(spread.shape, 0) == iota(spread.shape, 1)
    return jnp.sum(jnp.where(keep, spread, 0.0), axis=0, keepdims=True)


def two_rows(first, second):
    lines = iota((16, first.shape[1]), 0)
    return jnp.where(lines == 0, first, jnp.where(lines == 1, second, 0.0)).astype(BF16)


def plan(parent, counts, ends, token, prob, uniform, vec, which):
    shape = parent.shape
    lines, lanes = iota((1, 128), 0), iota((1, 128), 1)
    total = jnp.zeros((1, 128), F32)
    before = (iota((128, 128), 0) < iota((128, 128), 1)).astype(F32).astype(BF16)
    order, reads = [], []
    for t in range(shape[0]):
        second = lanes >= 64
        slot = jnp.where(second, lanes - 64, lanes)
        live = slot < jnp.where(second, counts[2 * t + 1], counts[2 * t])
        end = slot == jnp.where(second, ends[2 * t + 1], ends[2 * t])
        up = parent[t : t + 1, :] - t * 128
        root = up == lanes
        child = jnp.where(live & jnp.logical_not(root), up.astype(F32), -1.0)
        column = to_column(child, 128)
        hit = (column == iota((128, 128), 1).astype(F32)).astype(F32)
        needed = jnp.max(hit, axis=0, keepdims=True)
        plain = jnp.where(end, 0.0, needed)
        vec[0 + t : 1 + t, :] = up.astype(F32)
        vec[16 + t : 17 + t, :] = plain
        vec[24 + t : 25 + t, :] = jnp.where(end, jnp.where(second, 2 * t + 1, 2 * t), -1).astype(F32)
        vec[32 + t : 33 + t, :] = jnp.where(root, 1.0, jnp.where(live, 0.0, 1.0))
        vec[40 + t : 41 + t, :] = root.astype(F32)
        within = jnp.dot(
            jnp.broadcast_to(plain, (16, 128)).astype(BF16), before, preferred_element_type=F32
        )[0:1, :]
        vec[56 + t : 57 + t, :] = within + total
        total = total + jnp.sum(plain, axis=1, keepdims=True)
    vec[8:16, :] = token[...].astype(F32)
    vec[48:56, :] = jnp.log(prob[...]) + jnp.log(uniform[...])
    size = jnp.max(total).astype(jnp.int32)
    which[0] = sum(jnp.where(size > NZ * (cap - 2), 1, 0) for cap in BLOCKS[:-1])


def kernel(
    cap, vec, own, head, out_s, out_e,
    w, hid, comp, acc, pick, tok, pp, reach, rq, rs, sq, ss,
    scores, tpk, send_a, recv_a, send_b, recv_b, ext,
    loc, gs, gr, pr, qs, qr, ps, pq, a_s, a_r, b_s, b_r, e_s, e_r,
):
    rows = cap * NZ
    nodes = tok.shape[1]
    groups = nodes // 128
    width = head.shape[1]
    tiles = width // TILE
    x, y = lax.axis_index("gx_0"), lax.axis_index("gx_1")
    c, z = lax.axis_index("gx_2"), lax.axis_index("gy")
    gx = (x * NY + y) * NC + c
    first = c == 0

    load_w = pltpu.make_async_copy(head, w, loc.at[1])
    load_w.start()
    own_rows = pl.ds(pl.multiple_of(gx * 2 * HALF, 2 * HALF), 2 * HALF)
    load_own = pltpu.make_async_copy(own, hid.at[own_rows], loc.at[0])
    load_own.start()

    xs = [lax.rem(x + d, NX) for d in range(NX)]
    ys = [lax.rem(y + d, NY) for d in range(NY)]
    peers = []
    for dx in (2, 1, 3, 0):
        for dy in (2, 1, 3, 0):
            for other in (1, 0):
                if dx or dy or other:
                    core = 1 - c if other else c
                    peers.append(((xs[dx] * NY + ys[dy]) * NC + core, (xs[dx], ys[dy], core, z)))
    stack = [(p, (x, y, c, p)) for p in (lax.rem(z + d, NZ) for d in (4, 3, 5, 2, 6, 1, 7))]

    barrier = pltpu.get_barrier_semaphore()
    near = [(xs[2], y, c, z), (x, ys[2], c, z), (xs[1], y, c, z), (xs[3], y, c, z)]
    near += [(x, ys[1], c, z), (x, ys[3], c, z), (x, y, 1 - c, z)]
    near += [(x, y, c, lax.rem(z + d, NZ)) for d in (1, NZ - 1)]
    for to in near:
        pl.semaphore_signal(barrier, inc=1, device_id=to, device_id_type=AT)
    load_own.wait()
    pl.semaphore_wait(barrier, len(near))

    places = {}

    def block(da, db, h, core):
        straight = core == 0
        bx = lax.rem(x + jnp.where(straight, da, db), NX)
        by = lax.rem(y + jnp.where(straight, db, da), NY)
        at = (((bx * NY + by) * NC + core) * 2 + h) * HALF
        return pl.ds(pl.multiple_of(at, HALF), HALF)

    for da in range(4):
        for db in range(4):
            for h in range(2):
                places[da, db, h] = block(da, db, h, c)

    sent = []
    counts = {}

    def chip(axis, step):
        along_x = first if axis == 0 else jnp.logical_not(first)
        tx = lax.rem(x + jnp.where(along_x, step, 0) + NX, NX)
        ty = lax.rem(y + jnp.where(along_x, 0, step) + NY, NY)
        return (tx, ty, c, z)

    chips = {(axis, step): chip(axis, step) for axis in range(2) for step in (1, -1, 2)}
    partner = (x, y, 1 - c, z)

    def push(da, db, h, arrival, to):
        here = hid.at[places[da, db, h]]
        n = counts.get(h, 0)
        counts[h] = n + 1
        copy = pltpu.make_async_remote_copy(
            src_ref=here, dst_ref=here, send_sem=gs.at[h, n], recv_sem=arrival,
            device_id=to, device_id_type=AT,
        )
        copy.start()
        sent.append(copy)

    def send(da, db, h, axis, step):
        ra = (da - step) % 4 if axis == 0 else da
        rb = (db - step) % 4 if axis == 1 else db
        push(da, db, h, gr.at[h, ra, rb], chips[axis, step])

    def share(da, db, h):
        push(da, db, h, pr.at[h, da, db], partner)

    def landed(ref, arrival):
        pltpu.make_async_remote_copy(
            src_ref=ref, dst_ref=ref, send_sem=gs.at[0, 0], recv_sem=arrival,
            device_id=partner, device_id_type=AT,
        ).wait_recv()

    def arrive(da, db, h):
        landed(hid.at[places[da, db, h]], gr.at[h, da, db])

    def arrive_partner(dx):
        for h in range(2):
            for k in range(4):
                da, db = jnp.where(first, k, dx), jnp.where(first, dx, k)
                landed(hid.at[block(da, db, h, 1 - c)], pr.at[h, da, db])

    sign = (1, -1)
    away = (2, 3, 1)

    def level_0():
        for h in range(2):
            for step in (2, 1, -1):
                send(0, 0, h, 0, step)
            for step in (1, -1):
                send(0, 0, h, 1, step)
        for h in range(2):
            share(0, 0, h)

    def level_1():
        for h in range(2):
            s = sign[h]
            for da in (s % 4, -s % 4, 2):
                arrive(da, 0, h)
                send(da, 0, h, 1, s)
                send(da, 0, h, 1, -s)
            arrive(0, -s % 4, h)
            send(0, -s % 4, h, 1, s)
            arrive(0, s % 4, h)
        for h in range(2):
            for da in away:
                share(da, 0, h)
            for db in (3, 1):
                share(0, db, h)

    def level_2():
        for h in range(2):
            s = sign[h]
            for da in (3, 1, 2):
                arrive(da, -s % 4, h)
                send(da, -s % 4, h, 1, s)
        for h in range(2):
            s = sign[h]
            arrive(0, 2, h)
            share(0, 2, h)
            for da in (3, 1, 2):
                share(da, -s % 4, h)
                arrive(da, s % 4, h)
                share(da, s % 4, h)

    def level_3():
        for da in (3, 1, 2):
            for h in range(2):
                arrive(da, 2, h)
                share(da, 2, h)

    level_0()

    per = cap - 2
    order = vec[56:64, :]
    home = jnp.zeros_like(order)
    for i in range(1, NZ):
        home = home + (order >= float(i * per)).astype(F32)
    spot = home * cap + (order - home * per) + 2.0
    ends = vec[24:32, :]
    pair = jnp.floor(ends * 0.5)
    end_spot = jnp.where(ends >= 0.0, pair * cap + (ends - 2.0 * pair), -1.0)
    pos = jnp.where(vec[16:24, :] > 0.0, spot, end_spot)
    pos_id = pos.astype(jnp.int32)

    def mark(j, _):
        at = pl.ds(pl.multiple_of(j * 64, 64), 64)
        for t in range(groups):
            same = iota((64, 128), 0) + j * 64 == pos_id[t : t + 1, :]
            pick[at, t * 128 : (t + 1) * 128] = same.astype(F32).astype(BF16)
        return 0

    lax.fori_loop(0, rows // 64, mark, 0)
    level_1()

    token = vec[8:16, :].astype(jnp.int32) - gx * width

    def token_rows(j, _):
        at = pl.ds(pl.multiple_of(j * 128, 128), 128)
        for t in range(groups):
            same = iota((128, 128), 0) + j * 128 == token[t : t + 1, :]
            tok[at, t * 128 : (t + 1) * 128] = same.astype(F32).astype(BF16)
        return 0

    lax.fori_loop(0, width // 128, token_rows, 0)
    upper = jnp.floor(pos * (1.0 / 32.0))
    lower = pos - 32.0 * upper
    parents = vec[0:8, :].astype(jnp.int32)
    for t in range(groups):
        hit = (iota((128, 128), 0) == parents[t : t + 1, :]).astype(F32).astype(BF16)
        both = two_rows(upper[t : t + 1, :], lower[t : t + 1, :])
        got = jnp.dot(both, hit, preferred_element_type=F32)
        pp[t : t + 1, :] = got[0:1, :] * 32.0 + got[1:2, :]
    group = gx // 4
    up = vec[pl.ds(group, 1), :].astype(jnp.int32)
    line, lane_ids = iota((128, 128), 0), iota((128, 128), 1)
    reach[...] = jnp.where(line == up, 1.0, jnp.where(line == lane_ids, 1.0, 0.0))

    def spread(_, carry):
        now = reach[...].astype(BF16)
        reach[...] = jnp.minimum(jnp.dot(now, now, preferred_element_type=F32), 1.0)
        return carry

    lax.fori_loop(0, 6, spread, 0)

    level_2()

    def select(group_of, start):
        quarter = nodes // NX
        for dx in group_of:
            arrive_partner(dx)

        def body(j, _):
            lane = pl.ds(pl.multiple_of(j * TILE, TILE), TILE)
            got = None if start else comp[:, lane].astype(F32)
            for dx in group_of:
                at = pl.ds(pl.multiple_of(xs[dx] * quarter, quarter), quarter)
                new = jnp.dot(pick[:, at], hid[at, lane], preferred_element_type=F32)
                got = new if got is None else got + new
            comp[:, lane] = got.astype(BF16)
            return 0

        lax.fori_loop(0, hid.shape[1] // TILE, body, 0)

    select((0,), True)
    level_3()
    load_w.wait()
    select((3, 1, 2), False)

    def lanes_of(j):
        return pl.ds(pl.multiple_of(j * TILE, TILE), TILE)

    def quantize(v, m, j):
        top = jnp.maximum(jnp.max(jnp.abs(v), axis=0, keepdims=True), 1e-30)
        ss[m, j] = top * (1.0 / 32767.0)
        v = jnp.round(v * (32767.0 / top))
        v = jnp.concatenate([v[:, i : i + 128] for i in range(0, TILE, 128)], axis=0)
        sq[m, j] = v.astype(jnp.int32).astype(jnp.int16)

    above, below = (x, y, c, lax.rem(z + 1, NZ)), (x, y, c, lax.rem(z + NZ - 1, NZ))

    def ring_copies(m, j, way):
        to = above if (way == 0) == (m < LONG) else below
        return (
            pltpu.make_async_remote_copy(
                src_ref=sq.at[m, j], dst_ref=rq.at[m, j], send_sem=qs.at[m, j],
                recv_sem=qr.at[m, j], device_id=to, device_id_type=AT),
            pltpu.make_async_remote_copy(
                src_ref=ss.at[m, j], dst_ref=rs.at[m, j], send_sem=ps.at[m, j],
                recv_sem=pq.at[m, j], device_id=to, device_id_type=AT),
        )

    def rows_of(steps):
        d = lax.rem(z + steps + NZ, NZ)
        return pl.ds(pl.multiple_of(d * cap, 8), cap)

    def goal(m, way):
        s = 1 if way == 0 else -1
        return s * (LONG - m) if m < LONG else -s * (NZ - 1 - m)

    def forward(v, m, j, way):
        quantize(v, m, j)
        for copy in ring_copies(m, j, way):
            copy.start()

    def arrived(m, j, way):
        for copy in ring_copies(m, j, way):
            copy.wait_recv()
        v = rq[m, j].astype(jnp.int32).astype(F32)
        v = jnp.concatenate([v[i * cap : (i + 1) * cap] for i in range(TILE // 128)], axis=1)
        return v * rs[m, j]

    def multiply(jj, _):
        for way in range(2):
            j = jj * 2 + way
            acc[:, lanes_of(j)] = jnp.dot(comp[...], w[:, lanes_of(j)], preferred_element_type=F32)
            for m in (0, LONG):
                forward(acc[rows_of(goal(m, way)), lanes_of(j)], m, j, way)
        return 0

    lax.fori_loop(0, tiles // 2, multiply, 0)

    for hop in range(1, LONG):
        def pass_on(jj, _, hop=hop):
            for way in range(2):
                j = jj * 2 + way
                for m in (hop, LONG + hop):
                    if m < NZ - 1:
                        got = arrived(m - 1, j, way)
                        forward(got + acc[rows_of(goal(m, way)), lanes_of(j)], m, j, way)
            return 0

        lax.fori_loop(0, tiles // 2, pass_on, 0)

    tpk[...] = jnp.zeros_like(tpk)

    def finish(jj, _):
        for way in range(2):
            j = jj * 2 + way
            v = acc[rows_of(0), lanes_of(j)] + arrived(NZ - 2, j, way) + arrived(LONG - 1, j, way)
            scores[:, lanes_of(j)] = v
            high = v.astype(BF16).astype(F32)
            rest = v - high
            middle = rest.astype(BF16).astype(F32)
            pieces = jnp.concatenate([high, middle, rest - middle], axis=0).astype(BF16)
            got = jnp.dot(pieces, tok[lanes_of(j), :], preferred_element_type=F32)
            tpk[...] += got[0:cap] + got[cap : 2 * cap] + got[2 * cap : 3 * cap]
        return 0

    lax.fori_loop(0, tiles // 2, finish, 0)

    ext[z] = scores[0:2, :]
    ext_copies = [
        pltpu.make_async_remote_copy(
            src_ref=ext.at[z], dst_ref=ext.at[z], send_sem=e_s.at[k],
            recv_sem=e_r.at[z], device_id=to, device_id_type=AT)
        for k, (_, to) in enumerate(stack)
    ]
    for copy in ext_copies:
        copy.start()

    top = jnp.max(scores[...], axis=1, keepdims=True)
    total = jnp.sum(jnp.exp(scores[...] - top), axis=1, keepdims=True)
    top_row, total_row = to_row(top, 128), to_row(total, 128)
    base = (z * cap).astype(F32)
    places_here = iota((cap, 128), 0).astype(F32) + base
    for t in range(groups):
        held = places_here == pp[t : t + 1, :]
        target = jnp.sum(
            jnp.where(held, tpk[:, t * 128 : (t + 1) * 128], 0.0), axis=0, keepdims=True
        )
        send_a[t] = jnp.concatenate([target, top_row, total_row], axis=1)
    recv_a[gx] = send_a[group]
    plane_copies = [
        pltpu.make_async_remote_copy(
            src_ref=send_a.at[p // 4], dst_ref=recv_a.at[gx], send_sem=a_s.at[k],
            recv_sem=a_r.at[gx], device_id=to, device_id_type=AT)
        for k, (p, to) in enumerate(peers)
    ]
    for copy in plane_copies:
        copy.start()

    for copy in sent:
        copy.wait_send()

    def ring_drain(jj, _):
        for way in range(2):
            for m in range(NZ - 1):
                for copy in ring_copies(m, jj * 2 + way, way):
                    copy.wait_send()
        return 0

    lax.fori_loop(0, tiles // 2, ring_drain, 0)
    for k, (p, to) in enumerate(reversed(peers)):
        landed(recv_a.at[p], a_r.at[p])
    parts = [recv_a[k] for k in range(PLANE)]
    tops = [p[:, 128:256] for p in parts]
    while len(tops) > 1:
        tops = [jnp.maximum(a, b) for a, b in zip(tops[::2], tops[1::2])]
    sums = [p[:, 256:384] * jnp.exp(p[:, 128:256] - tops[0]) for p in parts]
    wanted = [p[:, 0:128] for p in parts]
    while len(sums) > 1:
        sums = [a + b for a, b in zip(sums[::2], sums[1::2])]
        wanted = [a + b for a, b in zip(wanted[::2], wanted[1::2])]
    used = iota((1, 128), 1) < cap
    log_total = jnp.where(used, tops[0] + jnp.log(jnp.where(used, sums[0], 1.0)), 0.0)
    column = to_column(log_total, cap)
    here = places_here == pp[pl.ds(group, 1), :]
    mine_part = wanted[0] - jnp.sum(jnp.where(here, column, 0.0), axis=0, keepdims=True)
    send_b[...] = jnp.concatenate([mine_part, log_total], axis=1)
    recv_b[z] = send_b[...]
    b_copies = [
        pltpu.make_async_remote_copy(
            src_ref=send_b, dst_ref=recv_b.at[z], send_sem=b_s.at[k],
            recv_sem=b_r.at[z], device_id=to, device_id_type=AT)
        for k, (_, to) in enumerate(stack)
    ]
    for copy in b_copies:
        copy.start()
    for copy in plane_copies + ext_copies:
        copy.wait_send()
    for p, _ in stack:
        landed(ext.at[p], e_r.at[p])
    for p, _ in reversed(stack):
        landed(recv_b.at[p], b_r.at[p])

    margin = recv_b[0][:, 0:128]
    for k in range(1, NZ):
        margin = margin + recv_b[k][:, 0:128]
    margin = margin - vec[pl.ds(48 + group, 1), :]
    spare = vec[pl.ds(32 + group, 1), :] > 0.0
    climb = to_column(jnp.where(vec[pl.ds(40 + group, 1), :] > 0.0, BIG, margin), 128)
    least = jnp.min(jnp.where(reach[...] > 0.0, climb, BIG), axis=0, keepdims=True)
    both = jnp.where(
        iota((8, 128), 0) == 0,
        jnp.where(spare, 0.0, margin),
        jnp.where(spare, 0.0, least),
    )
    both = pltpu.roll(both, lax.rem(128 - 2 * HALF * lax.rem(gx, 4), 128), axis=1)
    out_s[...] = both
    lane = iota((1, 128), 1)
    for k in range(NZ):
        line = recv_b[k][:, 128:256]
        low = jnp.sum(jnp.where(lane == 0, line, 0.0), axis=1, keepdims=True)
        high = jnp.sum(jnp.where(lane == 1, line, 0.0), axis=1, keepdims=True)
        out_e[2 * k : 2 * k + 2, :] = ext[k] - jnp.where(iota((2, 1), 0) == 0, low, high)
    for copy in b_copies:
        copy.wait_send()


def fused(cap, number, vec, hidden, head):
    depth, width = head.shape
    nodes = hidden.shape[0] * PLANE
    rows, tiles, hops = cap * NZ, width // TILE, NZ - 1
    dma = pltpu.SemaphoreType.DMA
    vmem = pl.BlockSpec(memory_space=pltpu.VMEM)
    far = pl.BlockSpec(memory_space=pl.ANY)
    return pl.pallas_call(
        functools.partial(kernel, cap),
        out_shape=(
            jax.ShapeDtypeStruct((8, 128), F32),
            jax.ShapeDtypeStruct((2 * NZ, width), F32),
        ),
        in_specs=[vmem, far, far],
        out_specs=(vmem, vmem),
        scratch_shapes=[
            pltpu.VMEM((depth, width), BF16),
            pltpu.VMEM((nodes, depth), BF16),
            pltpu.VMEM((rows, depth), BF16),
            pltpu.VMEM((rows, width), F32),
            pltpu.VMEM((rows, nodes), BF16),
            pltpu.VMEM((width, nodes), BF16),
            pltpu.VMEM((8, 128), F32),
            pltpu.VMEM((128, 128), F32),
            pltpu.VMEM((hops, tiles, TILE // 128 * cap, 128), jnp.int16),
            pltpu.VMEM((hops, tiles, 1, TILE), F32),
            pltpu.VMEM((hops, tiles, TILE // 128 * cap, 128), jnp.int16),
            pltpu.VMEM((hops, tiles, 1, TILE), F32),
            pltpu.VMEM((cap, width), F32),
            pltpu.VMEM((cap, nodes), F32),
            pltpu.VMEM((nodes // 128, 1, 384), F32),
            pltpu.VMEM((PLANE, 1, 384), F32),
            pltpu.VMEM((1, 256), F32),
            pltpu.VMEM((NZ, 1, 256), F32),
            pltpu.VMEM((NZ, 2, width), F32),
            dma((2,)),
            dma((2, 31)),
            dma((2, 4, 4)),
            dma((2, 4, 4)),
            dma((hops, tiles)),
            dma((hops, tiles)),
            dma((hops, tiles)),
            dma((hops, tiles)),
            dma((PLANE,)),
            dma((PLANE,)),
            dma((NZ,)),
            dma((NZ,)),
            dma((NZ,)),
            dma((NZ,)),
        ],
        compiler_params=pltpu.CompilerParams(
            collective_id=number, has_side_effects=True, vmem_limit_bytes=67043328
        ),
        name=f"head_{cap}",
    )(vec, hidden, head)


def local(hidden, lm_head, parent, draft_token, draft_prob, uniforms, node_count, accepted_end):
    lines = (parent.shape[0] // 128, 128)
    vmem, smem = pl.BlockSpec(memory_space=pltpu.VMEM), pl.BlockSpec(memory_space=pltpu.SMEM)
    vec, which = pl.pallas_call(
        plan,
        out_shape=(
            jax.ShapeDtypeStruct((64, 128), F32),
            jax.ShapeDtypeStruct((1,), jnp.int32),
        ),
        in_specs=[vmem, smem, smem, vmem, vmem, vmem],
        out_specs=(vmem, smem),
        name="plan",
    )(
        parent.reshape(lines), node_count, accepted_end, draft_token.reshape(lines),
        draft_prob.reshape(lines), uniforms.reshape(lines),
    )

    def branch(i, *args):
        small, extra = fused(BLOCKS[i], i, *args)
        return small[0, : 2 * HALF], small[1, : 2 * HALF], extra

    branches = [functools.partial(branch, i) for i in range(len(BLOCKS))]
    return lax.switch(which[0], branches, vec, hidden, lm_head)


def solution(mesh):
    finer = Mesh(mesh.devices.reshape(NX, NY, NC, NZ), ALL)
    placed = (P(GX, "gy"), P("gy", GX), P(), P(), P(), P(), P(), P())
    return jax.shard_map(
        local, mesh=finer, in_specs=placed, out_specs=(P(GX), P(GX), P(None, GX)), check_vma=False
    )
```
